32 devices in a mesh: team: 8 (over z, core), member: 4 (over y, x).
Axes of the slice: x: 2, y: 2, z: 4, core: 2. Of those that a mesh axis runs over, the one named last changes fastest.
Arguments:
- state_start: float32 [24, 512, 512], P(None, 'team', 'member'), may hold values from -6 to 6
- state_section: float32 [24, 512, 512], P(None, 'team', 'member'), may hold values from -6 to 6
- velocity: float32 [2, 512, 512], P(None, 'team', 'member'), may hold values from -3 to 3
- diffusivity: float32 [24], replicated, may hold values from 0.05 to 0.5
- flame_cells: int32 [32, 128], P(('team', 'member')), may hold values from 0 to 8191, as said below
- block_team: int32 [32, 1], replicated, may hold values from 0 to 7; in each aligned block of 4 rows (0 to 3, 4 to 7, ...) at most 2 rows name the same one
- w_in: bfloat16 [8, 4, 1600, 24], P('team', 'member'), may hold values from -1.25 to 1.25
- w_mid: bfloat16 [8, 4, 800, 1600], P('team', 'member'), may hold values from -0.15625 to 0.15625
- w_low: bfloat16 [8, 4, 400, 800], P('team', 'member'), may hold values from -0.21875 to 0.21875
- w_out: bfloat16 [8, 4, 24, 400], P('team', 'member'), may hold values from -0.3125 to 0.3125
Outputs:
- source_rates: float32 [24, 512, 512], P(None, 'team', 'member')
- new_state: float32 [24, 512, 512], P(None, 'team', 'member')
The draws below stay inside these ranges and needn't reach their ends.
Inputs may be any that keep to these rules, and one draw needn't show every extreme that they name: `flame_cells`: the 128 entries of the rows of one device (rows d * 1 to d + 1 - 1) are distinct cells of that device's tile, given as i * 128 + j. `block_team`: in each aligned block of 4 rows (the flame blocks of one index of team) no regime appears more than 2 times.
All inputs are finite; a program needn't handle non-finite values.
Results may differ from the reference program's by a relative error of at most 0.0017.
The reference program's roundings to bfloat16 on the way (of `inputs`, `hidden_one`, `hidden_two` and `hidden_three`) count: a program that leaves them out, or rounds other values in their place, can miss the bound.
Values may be sent and summed in bfloat16 or wider, within the bound.
A program may use at most 64 MiB of HBM per device.

```python
import math
import jax
import jax.numpy as jnp
import numpy as np
from jax import lax

F = 24
H1 = 1600
H2 = 800
H3 = 400
BLOCK = 128
BLK_DEV = 1
CAP = 2
CX = 64
CY = 128
NX = 512
NY = 512
REGIMES = 8
NETS = 4
BLOCKS = 32
N_TEAM = 8
N_MEMBER = 4


def draw_flame_cells(key, part):
    owners = N_TEAM * N_MEMBER
    key_list = jax.random.split(jax.random.fold_in(key, 11), owners)

    def pick_cells(subkey):
        shuffled = jax.random.permutation(subkey, CX * CY)
        return shuffled[:BLK_DEV * BLOCK]
    flame_rows = jax.vmap(pick_cells)(key_list)
    return flame_rows.reshape(BLK_DEV * owners, BLOCK).astype(jnp.int32)


def level_of(rng, extent, cuts, low, top_value):
    def one(axis_at, blocks):
        steps = jax.random.uniform(jax.random.fold_in(jax.random.fold_in(rng, 6), axis_at), (blocks,), jnp.float32, low / len(cuts), top_value / len(cuts))
        return jnp.repeat(jnp.exp(steps), extent[axis_at] // blocks).reshape((-1,) + (1,) * (len(extent) - axis_at - 1))

    level = one(*cuts[0])
    for cut in cuts[1:]:
        level = level * one(*cut)
    return level


def shared_out(key, own, number, rows, number_of, top, most, lean):
    ranking = jax.random.permutation(key, number_of)
    packed, ordinary = portions_of(number_of, rows * top, most, lean, True), portions_of(number_of, rows * top, most, lean, False)
    places = jnp.arange(number_of)

    def named(tallies, rotation):
        used = int((tallies > 0).sum())
        fixed = max(1, used // 4)
        moved = fixed + (places - fixed + rotation * (used - fixed)) % max(1, number_of - fixed)
        return jnp.zeros((number_of,), jnp.int32).at[ranking[jnp.where(places < fixed, places, moved)]].set(jnp.asarray(tallies, jnp.int32))

    tallies = jnp.where(number % 4 == 0, named(packed, number // 4), named(ordinary, number - number // 4 - 1))
    mixed = jax.random.permutation(jax.random.fold_in(own, 3), number_of)
    source_of, sink = mixed[0:number_of // 2 * 2:2], mixed[1:number_of // 2 * 2:2]
    margin = jnp.minimum(tallies[source_of] - 1, most - tallies[sink]) // 2
    margin = jnp.where((source_of == ranking[0]) | (sink == ranking[0]) | (tallies[sink] == 0), 0, jnp.maximum(margin, 0))
    moved = jax.random.randint(jax.random.fold_in(own, 4), (number_of // 2,), 0, 1 << 20) % (margin + 1)
    tallies = tallies.at[source_of].add(-moved).at[sink].add(moved)
    items = jnp.searchsorted(jnp.cumsum(tallies), jnp.arange(rows * top), side="right").astype(jnp.int32)
    listing = items.reshape(top, rows).T
    listing = listing[jax.random.permutation(jax.random.fold_in(own, 1), rows)]
    rotation = jax.random.randint(jax.random.fold_in(own, 2), (rows, 1), 0, top)
    return jnp.take_along_axis(listing, (jnp.arange(top)[None, :] + rotation) % top, axis=1)


def portions_of(amount, total, bound, lean, full):
    portions = [(1 << 20) // math.isqrt(standing ** lean) + 1 for standing in range(1, amount + 1)]
    largest = bound if full else min(bound, max(-(-total // amount), total * portions[0] // sum(portions)))
    least = 1 if total - largest >= amount - 1 else 0
    counts, spare = [largest] + [least] * (amount - 1), total - largest - least * (amount - 1)
    while spare > 0:
        candidates = [i for i in range(1, amount) if counts[i] < largest] or [i for i in range(1, amount) if counts[i] < bound]
        pool, remaining = sum([portions[i] for i in candidates]), spare
        for i in candidates:
            extra = min(bound - counts[i], max(1, remaining * portions[i] // pool), spare)
            counts[i] = counts[i] + extra
            spare = spare - extra
    return np.array(counts)


def normal_values(own_key, shape, width, bound, cuts=(), held_as=jnp.bfloat16):
    array = width * jax.random.normal(own_key, shape, jnp.float32)
    if cuts:
        array = array * level_of(own_key, shape, cuts, -0.22, 0.18)
    return jnp.clip(array, -bound, bound).astype(held_as)


def setup_inputs(seed: int = 0) -> dict:
    streams_of = jax.random.split(jax.random.key(seed), 11)
    state_start = normal_values(streams_of[0], (F, NX, NY), 1.0, 6.0, ((1, 8), (2, 4)), jnp.float32)
    state_section = normal_values(streams_of[1], (F, NX, NY), 1.0, 6.0, ((1, 8), (2, 4)), jnp.float32)
    velocity = normal_values(streams_of[2], (2, NX, NY), 0.7, 3.0, ((1, 8), (2, 4)), jnp.float32)
    diffusivity = jnp.clip(jnp.exp(jax.random.uniform(streams_of[3], (F,), jnp.float32, math.log(0.05), math.log(0.5))), 0.05, 0.5)
    flame_cells = draw_flame_cells(jax.random.fold_in(streams_of[10], 71), 0)
    block_team_keys = jax.random.split(jax.random.fold_in(streams_of[5], 1), BLOCKS // (N_MEMBER * BLK_DEV))
    block_team_turns = jax.random.permutation(jax.random.fold_in(streams_of[5], 3), BLOCKS // (N_MEMBER * BLK_DEV))
    block_team = jax.vmap(lambda own, number: shared_out(jax.random.fold_in(streams_of[5], 2), own, number, N_MEMBER * BLK_DEV, N_TEAM, 1, CAP, 2))(block_team_keys, block_team_turns).reshape((BLOCKS, 1))
    w_in = normal_values(streams_of[6], (REGIMES, NETS, H1, F), F ** -0.5, 1.25, ((0, 8), (1, 4)))
    w_mid = normal_values(streams_of[7], (REGIMES, NETS, H2, H1), H1 ** -0.5, 0.15625, ((0, 8), (1, 4)))
    w_low = normal_values(streams_of[8], (REGIMES, NETS, H3, H2), H2 ** -0.5, 0.21875, ((0, 8), (1, 4)))
    w_out = normal_values(streams_of[9], (REGIMES, NETS, F, H3), H3 ** -0.5, 0.3125, ((0, 8), (1, 4)))
    return dict(state_start=state_start, state_section=state_section, velocity=velocity, diffusivity=diffusivity, flame_cells=flame_cells, block_team=block_team, w_in=w_in, w_mid=w_mid, w_low=w_low, w_out=w_out)


TIME_STEP = 0.25


def flow_operator(state_section, velocity, diffusivity):
    plus_x = jnp.roll(state_section, -1, axis=1)
    minus_x = jnp.roll(state_section, 1, axis=1)
    plus_y = jnp.roll(state_section, -1, axis=2)
    minus_y = jnp.roll(state_section, 1, axis=2)
    spread = diffusivity[:, None, None] * (plus_x + minus_x + plus_y + minus_y - 4.0 * state_section)
    advect = 0.5 * velocity[0][None] * (plus_x - minus_x) + 0.5 * velocity[1][None] * (plus_y - minus_y)
    return spread - advect


def network_sum(states, weight_in, weight_mid, weight_low, weight_out):
    highest = lax.Precision.HIGHEST
    layer_one = jnp.einsum("nhf,fk->nhk", weight_in.astype(jnp.float32), states.astype(jnp.float32), precision=highest)
    hidden_one = jax.nn.silu(layer_one).astype(jnp.bfloat16)
    layer_two = jnp.einsum("nih,nhk->nik", weight_mid.astype(jnp.float32), hidden_one.astype(jnp.float32), precision=highest)
    hidden_two = jax.nn.silu(layer_two).astype(jnp.bfloat16)
    layer_three = jnp.einsum("nji,nik->njk", weight_low.astype(jnp.float32), hidden_two.astype(jnp.float32), precision=highest)
    hidden_three = jax.nn.silu(layer_three).astype(jnp.bfloat16)
    return jnp.einsum("nfj,njk->fk", weight_out.astype(jnp.float32), hidden_three.astype(jnp.float32), precision=highest)


def reference(state_start, state_section, velocity, diffusivity, flame_cells, block_team, w_in, w_mid, w_low, w_out):
    block_ids = jnp.arange(BLOCKS, dtype=jnp.int32)
    owners = block_ids // BLK_DEV
    grid_x = ((owners // N_MEMBER)[:, None] * CX + flame_cells // CY).astype(jnp.int32)
    grid_y = ((owners % N_MEMBER)[:, None] * CY + flame_cells % CY).astype(jnp.int32)
    gathered = jnp.transpose(state_section[:, grid_x, grid_y], (1, 0, 2)).astype(jnp.bfloat16)

    def block_rates(inputs):
        states, regime = inputs
        return network_sum(states, w_in[regime], w_mid[regime], w_low[regime], w_out[regime])

    block_values = lax.map(block_rates, (gathered, block_team[:, 0]))
    source_rates = jnp.zeros(state_section.shape, jnp.float32).at[:, grid_x, grid_y].add(jnp.transpose(block_values, (1, 0, 2)))
    flow = flow_operator(state_section, velocity, diffusivity)
    new_state = 0.75 * state_start + 0.25 * (state_section + TIME_STEP * (flow + source_rates))
    return source_rates, new_state
```

```python
import functools

import jax
import jax.numpy as jnp
from jax import lax
from jax.experimental import pallas as pl
from jax.experimental.pallas import tpu as pltpu
from jax.sharding import PartitionSpec as P

CAP = 2
TIME_STEP = 0.25
GRANT = 24 << 20
GROUP = 4
ROWS = 400
MESH = pl.DeviceIdType.MESH
VMEM = pltpu.VMEM
F32 = jnp.float32
BF16 = jnp.bfloat16


def partner(index, flips):
    target = index
    bit = 1
    while bit <= flips:
        if flips & bit:
            target = target + bit - 2 * bit * lax.rem(index // bit, 2)
        bit *= 2
    return target


def split_cells(cells, rows_y):
    shift = rows_y.bit_length() - 1
    assert rows_y == 1 << shift
    return cells >> shift, cells & (rows_y - 1)


def row_mask(cells_x, rows_x):
    count = cells_x.shape[1]
    return lax.broadcasted_iota(jnp.int32, (rows_x, count), 0) == cells_x


def silu(x):
    half = 0.5 * x
    return half + half * jnp.tanh(half)


def greet(team, member, teams, members):
    barrier = pltpu.get_barrier_semaphore()
    for d in range(1, teams):
        pl.semaphore_signal(
            barrier, inc=1, device_id=(partner(team, d), member), device_id_type=MESH
        )
    for e in range(1, members):
        pl.semaphore_signal(
            barrier, inc=1, device_id=(team, partner(member, e)), device_id_type=MESH
        )
    return barrier


def flow_base(
    start_ref, section_ref, velocity_ref, spread_ref, halo_x_ref, halo_y_ref, base_ref
):
    fields, rows_x, rows_y = section_ref.shape
    lanes = lax.broadcasted_iota(jnp.int32, (rows_x, rows_y), 1)
    subs = lax.broadcasted_iota(jnp.int32, (rows_x, rows_y), 0)
    half_u = 0.5 * velocity_ref[0]
    half_v = 0.5 * velocity_ref[1]
    low_x = halo_x_ref[0].astype(F32)
    high_x = halo_x_ref[1].astype(F32)
    low_y = halo_y_ref[0].astype(F32)
    high_y = halo_y_ref[1].astype(F32)
    for f in range(fields):
        here = section_ref[f]
        plus_x = jnp.where(
            subs == rows_x - 1, high_x[f : f + 1], pltpu.roll(here, rows_x - 1, 0)
        )
        minus_x = jnp.where(subs == 0, low_x[f : f + 1], pltpu.roll(here, 1, 0))
        plus_y = jnp.where(
            lanes == rows_y - 1,
            pltpu.roll(high_y, rows_y - 1 - f, 1),
            pltpu.roll(here, rows_y - 1, 1),
        )
        edge = pltpu.roll(low_y, (rows_y - f) % rows_y, 1) if f else low_y
        minus_y = jnp.where(lanes == 0, edge, pltpu.roll(here, 1, 1))
        flow = (
            spread_ref[f] * (plus_x + minus_x + plus_y + minus_y - 4.0 * here)
            - half_u * (plus_x - minus_x)
            - half_v * (plus_y - minus_y)
        )
        base_ref[f] = 0.75 * start_ref[f] + 0.25 * (here + TIME_STEP * flow)


def network_sum(states, w_in, w_mid, w_low, w_out, hidden_one, hidden_two, hidden_three):
    count = states.shape[1]

    def layer(weight, source, target):
        total = weight.shape[0]
        for start in range(0, total, ROWS):
            size = min(ROWS, total - start)
            out = jnp.dot(weight[start : start + size, :], source, preferred_element_type=F32)
            target[start : start + size, :count] = silu(out).astype(BF16)

    layer(w_in, states, hidden_one)
    layer(w_mid.at[0, 0], hidden_one[:, :count], hidden_two)
    layer(w_low.at[0, 0], hidden_two[:, :count], hidden_three)
    return jnp.dot(w_out[0, 0], hidden_three[:, :count], preferred_element_type=F32)


def fused_kernel(
    teams,
    members,
    extra,
    section_hbm,
    start_hbm,
    velocity_hbm,
    cells_hbm,
    teams_hbm,
    spread_hbm,
    w_in_hbm,
    w_mid_hbm,
    w_low_hbm,
    w_out_hbm,
    own_ref,
    base_ref,
    flag_ref,
    section_ref,
    start_ref,
    velocity_ref,
    cells_ref,
    teams_ref,
    team_of,
    spread_ref,
    w_in_raw,
    w_in,
    w_mid,
    w_low,
    w_out,
    hidden_one,
    hidden_two,
    hidden_three,
    blocks,
    put,
    first_in,
    second_in,
    result,
    packed,
    back,
    chosen,
    got,
    edge_x,
    edge_y,
    halo_x,
    halo_y,
    rank_of,
    load_sem,
    send_b,
    recv_b,
    send_x,
    recv_x,
    send_r,
    recv_r,
    send_m,
    recv_m,
    send_h,
    recv_h,
):
    team = lax.axis_index("team")
    member = lax.axis_index("member")
    barrier = greet(team, member, teams, members)
    loads = []
    for k, (source, target) in enumerate(
        (
            (cells_hbm, cells_ref),
            (section_hbm, section_ref),
            (teams_hbm, team_of),
            (w_in_hbm, w_in_raw),
            (w_mid_hbm, w_mid),
            (w_low_hbm, w_low),
            (w_out_hbm, w_out),
            (teams_hbm, teams_ref),
            (spread_hbm, spread_ref),
            (velocity_hbm, velocity_ref),
            (start_hbm, start_ref),
        )
    ):
        copy = pltpu.make_async_copy(source, target, load_sem.at[k])
        copy.start()
        loads.append(copy)
    fields, rows_x, rows_y = section_ref.shape
    loads[0].wait()
    cells_x, cells_y = split_cells(cells_ref[...], rows_y)
    count = cells_x.shape[1]
    pick_y = (lax.broadcasted_iota(jnp.int32, (rows_y, count), 0) == cells_y).astype(F32)
    pick_x = row_mask(cells_x, rows_x)
    loads[1].wait()
    flat = section_ref[...].reshape(fields * rows_x, rows_y).astype(BF16)
    taken = jnp.dot(flat, pick_y.astype(BF16), preferred_element_type=F32)
    taken = taken.reshape(fields, rows_x, count)
    own = jnp.sum(jnp.where(pick_x[None], taken, 0.0), axis=1)
    blocks[member] = own.astype(BF16)
    pl.semaphore_wait(barrier, teams + members - 2)

    def remote(source, target, send, recv, device):
        copy = pltpu.make_async_remote_copy(
            src_ref=source,
            dst_ref=target,
            send_sem=send,
            recv_sem=recv,
            device_id=device,
            device_id_type=MESH,
        )
        copy.start()
        return copy

    swaps = []
    for e in range(members - 1, 0, -1):
        swaps.append(
            remote(
                blocks.at[member],
                blocks.at[member],
                send_b.at[e],
                recv_b.at[e],
                (team, partner(member, e)),
            )
        )

    edge_x[0] = section_ref[:, rows_x - 1, :].astype(BF16)
    edge_x[1] = section_ref[:, 0, :].astype(BF16)
    loads[2].wait()
    picks = []
    for d in range(teams):
        regime = partner(team, d)
        first = jnp.int32(0)
        second = jnp.int32(0)
        for q in range(members - 1, -1, -1):
            here = team_of[0, team * members + q] == regime
            second = jnp.where(here, first, second)
            first = jnp.where(here, q, first)
        picks.append((first, second))
    for copy in swaps:
        copy.wait_recv()
    first_in[0] = blocks[picks[0][0]]
    second_in[team] = blocks[picks[0][1]]
    firsts, seconds = {}, {}
    for d in range(1, teams):
        put[0, d] = blocks[picks[d][0]]
        firsts[d] = remote(
            put.at[0, d],
            first_in.at[d],
            send_x.at[0, d],
            recv_x.at[0, d],
            (partner(team, d), member),
        )
    for d in range(1, teams):
        put[1, d] = blocks[picks[d][1]]
        seconds[d] = remote(
            put.at[1, d],
            second_in.at[team],
            send_x.at[1, d],
            recv_x.at[1, d],
            (partner(team, d), member),
        )
    loads[3].wait()
    w_in[...] = w_in_raw[0, 0].T
    lanes = lax.broadcasted_iota(jnp.int32, (rows_x, rows_y), 1)
    low = jnp.zeros((rows_x, rows_y), F32)
    high = jnp.zeros((rows_x, rows_y), F32)
    for f in range(fields):
        plane = section_ref[f]
        here = lanes == f
        high = jnp.where(here, pltpu.roll(plane, (f + 1) % rows_y, 1), high)
        low = jnp.where(here, pltpu.roll(plane, f, 1) if f else plane, low)
    edge_y[0] = high.astype(BF16)
    edge_y[1] = low.astype(BF16)
    halos = []
    for k, (step, edge, halo, along) in enumerate(
        (
            (1, edge_x.at[0], halo_x.at[0], "team"),
            (-1, edge_x.at[1], halo_x.at[1], "team"),
            (1, edge_y.at[0], halo_y.at[0], "member"),
            (-1, edge_y.at[1], halo_y.at[1], "member"),
        )
    ):
        if along == "team":
            device = (lax.rem(team + step + teams, teams), member)
        else:
            device = (team, lax.rem(member + step + members, members))
        halos.append(remote(edge, halo, send_h.at[k], recv_h.at[k], device))

    found = jnp.int32(0)
    sources = [jnp.int32(0)] * extra
    for p in range(teams):
        held = jnp.int32(0)
        for q in range(members):
            held = held + (team_of[0, p * members + q] == team).astype(jnp.int32)
        twice = held > 1
        if extra < teams:
            rank_of[p] = jnp.minimum(found, extra - 1)
            for k in range(extra):
                sources[k] = jnp.where(
                    jnp.logical_and(twice, found == k), jnp.int32(p), sources[k]
                )
            found = found + twice.astype(jnp.int32)
        else:
            rank_of[p] = jnp.int32(p)
            sources[p] = jnp.int32(p)
    for copy in loads[4:7]:
        copy.wait()
    nets = (w_in, w_mid, w_low, w_out, hidden_one, hidden_two, hidden_three)
    returns = []
    for start in range(0, teams, GROUP):
        spots = range(start, min(start + GROUP, teams))
        for d in spots:
            if d:
                firsts[d].wait_recv()
        states = jnp.concatenate([first_in[d] for d in spots], axis=1)
        rates = network_sum(states, *nets)
        for k, d in enumerate(spots):
            piece = rates[:, k * count : (k + 1) * count]
            if d:
                result[0, d] = piece
                returns.append(
                    remote(
                        result.at[0, d],
                        back.at[team],
                        send_r.at[0, d],
                        recv_r.at[0, d],
                        (partner(team, d), member),
                    )
                )
            else:
                back[team] = piece
    for d in range(1, teams):
        seconds[d].wait_recv()
    for start in range(0, extra, GROUP):
        spots = range(start, min(start + GROUP, extra))
        states = jnp.concatenate([second_in[sources[k]] for k in spots], axis=1)
        rates = network_sum(states, *nets)
        for k, spot in enumerate(spots):
            packed[spot] = rates[:, k * count : (k + 1) * count]
    for d in range(1, teams):
        target = partner(team, d)
        result[1, d] = packed[rank_of[target]]
        returns.append(
            remote(
                result.at[1, d],
                back.at[teams + team],
                send_r.at[1, d],
                recv_r.at[1, d],
                (target, member),
            )
        )
    back[teams + team] = packed[rank_of[team]]

    loads[7].wait()
    blocks_all = teams * members
    row = teams_ref[...]
    hits = (lax.broadcasted_iota(jnp.int32, (teams, blocks_all), 0) == row).astype(F32)
    rows = lax.broadcasted_iota(jnp.int32, (blocks_all, teams), 0)
    groups = lax.broadcasted_iota(jnp.int32, (blocks_all, teams), 1)
    inside = jnp.logical_and(rows >= groups * members, rows < (groups + 1) * members)
    tally = jnp.dot(hits.astype(BF16), inside.astype(F32).astype(BF16), preferred_element_type=F32)
    seconds_of = jnp.sum(jnp.where(tally > 1.5, 1.0, 0.0), axis=1, keepdims=True)
    flag_ref[0] = (jnp.max(seconds_of) > extra + 0.5).astype(jnp.int32)

    for copy in loads[8:]:
        copy.wait()
    for copy in halos:
        copy.wait_recv()
    flow_base(start_ref, section_ref, velocity_ref, spread_ref, halo_x, halo_y, base_ref)
    where = []
    for q in range(members):
        regime = team_of[0, team * members + q]
        rank = jnp.int32(0)
        for other in range(q):
            rank = rank + (team_of[0, team * members + other] == regime).astype(jnp.int32)
        where.append(jnp.minimum(rank, CAP - 1) * teams + regime)
    for copy in returns:
        copy.wait_recv()
    for q in range(members):
        chosen[q] = back[where[q]]
    sends = []
    for e in range(members - 1, 0, -1):
        target = partner(member, e)
        sends.append(
            remote(chosen.at[target], got.at[e], send_m.at[e], recv_m.at[e], (team, target))
        )
    total = chosen[member]
    for e in range(1, members):
        sends[members - 1 - e].wait_recv()
        total = total + got[e]
    own_ref[...] = total
    for copy in swaps + list(firsts.values()) + list(seconds.values()) + halos + returns + sends:
        copy.wait_send()


def update_kernel(
    groups, cells_ref, rates_ref, base_ref, source_out, new_out, source_ref, new_ref, sems
):
    fields, rows_x, rows_y = base_ref.shape
    cells_x, cells_y = split_cells(cells_ref[...], rows_y)
    count = cells_x.shape[1]
    pick_x = row_mask(cells_x, rows_x)
    pick_y = (lax.broadcasted_iota(jnp.int32, (rows_y, count), 0) == cells_y).astype(F32)
    pick_y = pick_y.astype(BF16)
    pick_y = jnp.concatenate([pick_y, pick_y], axis=1)
    group = fields // groups
    copies = []
    for f in range(fields):
        spread_rates = jnp.where(pick_x, rates_ref[f : f + 1, :], 0.0)
        top = spread_rates.astype(BF16)
        rest = (spread_rates - top.astype(F32)).astype(BF16)
        source = lax.dot_general(
            jnp.concatenate([top, rest], axis=1),
            pick_y,
            (((1,), (1,)), ((), ())),
            preferred_element_type=F32,
        )
        source_ref[f] = source
        new_ref[f] = base_ref[f] + (0.25 * TIME_STEP) * source
        if (f + 1) % group == 0:
            span = pl.ds(f + 1 - group, group)
            for k, (held, out) in enumerate(((source_ref, source_out), (new_ref, new_out))):
                copy = pltpu.make_async_copy(held.at[span], out.at[span], sems.at[k, f // group])
                copy.start()
                copies.append(copy)
    for copy in copies:
        copy.wait()


def whole(space=VMEM):
    return pl.BlockSpec(memory_space=space)


def shards(
    state_start,
    state_section,
    velocity,
    diffusivity,
    flame_cells,
    block_team,
    w_in,
    w_mid,
    w_low,
    w_out,
):
    teams = lax.axis_size("team")
    members = lax.axis_size("member")
    fields, rows_x, rows_y = state_section.shape
    count = flame_cells.shape[1]
    dma = pltpu.SemaphoreType.DMA
    w_in = jnp.swapaxes(w_in, 2, 3)
    hidden = w_in.shape[3]
    wide = min(GROUP, teams) * count
    operands = (
        state_section,
        state_start,
        velocity,
        flame_cells,
        block_team.reshape(1, -1),
        diffusivity,
        w_in,
        w_mid,
        w_low,
        w_out,
    )

    def networks(extra, collective, name, operands):
        return pl.pallas_call(
            functools.partial(fused_kernel, teams, members, extra),
            out_shape=(
                jax.ShapeDtypeStruct((fields, count), F32),
                jax.ShapeDtypeStruct(state_section.shape, F32),
                jax.ShapeDtypeStruct((1,), jnp.int32),
            ),
            in_specs=[whole(pltpu.HBM)] * len(operands),
            out_specs=(whole(), whole(), whole(pltpu.SMEM)),
            scratch_shapes=[
                VMEM(state_section.shape, F32),
                VMEM(state_start.shape, F32),
                VMEM(velocity.shape, F32),
                VMEM(flame_cells.shape, jnp.int32),
                VMEM((1, teams * members), jnp.int32),
                pltpu.SMEM((1, teams * members), jnp.int32),
                pltpu.SMEM(diffusivity.shape, F32),
                VMEM(w_in.shape, BF16),
                VMEM((hidden, fields), BF16),
                VMEM(w_mid.shape, BF16),
                VMEM(w_low.shape, BF16),
                VMEM(w_out.shape, BF16),
                VMEM((hidden, wide), BF16),
                VMEM((w_mid.shape[2], wide), BF16),
                VMEM((w_low.shape[2], wide), BF16),
                VMEM((members, fields, count), BF16),
                VMEM((CAP, teams, fields, count), BF16),
                VMEM((teams, fields, count), BF16),
                VMEM((teams, fields, count), BF16),
                VMEM((CAP, teams, fields, count), F32),
                VMEM((extra, fields, count), F32),
                VMEM((CAP * teams, fields, count), F32),
                VMEM((members, fields, count), F32),
                VMEM((members, fields, count), F32),
                VMEM((2, fields, rows_y), BF16),
                VMEM((2, rows_x, rows_y), BF16),
                VMEM((2, fields, rows_y), BF16),
                VMEM((2, rows_x, rows_y), BF16),
                pltpu.SMEM((teams,), jnp.int32),
                dma((11,)),
                dma((members,)),
                dma((members,)),
                dma((CAP, teams)),
                dma((CAP, teams)),
                dma((CAP, teams)),
                dma((CAP, teams)),
                dma((members,)),
                dma((members,)),
                dma((4,)),
                dma((4,)),
            ],
            compiler_params=pltpu.CompilerParams(
                collective_id=collective, has_side_effects=True, vmem_limit_bytes=GRANT
            ),
            name=name,
        )(*[pltpu.with_memory_space_constraint(x, pltpu.HBM) for x in operands])

    extra = max(2, teams // 4)
    rates, base, full = networks(extra, 0, "networks", operands)
    rates = lax.cond(
        full[0] == 0,
        lambda rates, *operands: rates,
        lambda rates, *operands: networks(teams, 1, "general", operands)[0],
        rates,
        *operands,
    )
    groups = 6 if fields % 6 == 0 else fields
    return pl.pallas_call(
        functools.partial(update_kernel, groups),
        out_shape=(
            jax.ShapeDtypeStruct(state_section.shape, F32),
            jax.ShapeDtypeStruct(state_section.shape, F32),
        ),
        in_specs=[whole()] * 3,
        out_specs=(whole(pl.ANY), whole(pl.ANY)),
        scratch_shapes=[
            VMEM(state_section.shape, F32),
            VMEM(state_section.shape, F32),
            dma((2, groups)),
        ],
        compiler_params=pltpu.CompilerParams(vmem_limit_bytes=GRANT),
        name="update",
    )(flame_cells, rates, base)


def solution(mesh):
    grid = P(None, "team", "member")
    weights = P("team", "member", None, None)
    placed = (
        grid,
        grid,
        grid,
        P(),
        P(("team", "member"), None),
        P(),
        weights,
        weights,
        weights,
        weights,
    )
    return jax.shard_map(
        shards, mesh=mesh, in_specs=placed, out_specs=(grid, grid), check_vma=False
    )
```

```python
import functools

import jax
import jax.numpy as jnp
from jax import lax
from jax.experimental import pallas as pl
from jax.experimental.pallas import tpu as pltpu
from jax.sharding import PartitionSpec as P

CAP = 2
TIME_STEP = 0.25
GRANT = 24 << 20
GROUP = 4
FIRST = 4
MESH = pl.DeviceIdType.MESH
VMEM = pltpu.VMEM
F32 = jnp.float32
BF16 = jnp.bfloat16


def partner(index, flips):
    target = index
    bit = 1
    while bit <= flips:
        if flips & bit:
            target = target + bit - 2 * bit * lax.rem(index // bit, 2)
        bit *= 2
    return target


def split_cells(cells, rows_y):
    shift = rows_y.bit_length() - 1
    assert rows_y == 1 << shift
    return cells >> shift, cells & (rows_y - 1)


def row_mask(cells_x, rows_x):
    count = cells_x.shape[1]
    return lax.broadcasted_iota(jnp.int32, (rows_x, count), 0) == cells_x


def silu(x):
    half = 0.5 * x
    return half + half * jnp.tanh(half)


def straight(teams, members):
    order = [(d, e) for d in range(4, teams, 2) for e in range(members)]
    order += [(0, e) for e in range(1, members)]
    order += [(1, e) for e in range(members)] if teams > 1 else []
    order += [(2, e) for e in range(members)] if teams > 2 else []
    return order


def greeted(teams, members):
    order = straight(teams, members)
    return order + [(d, 0) for d in range(1, teams) if (d, 0) not in order]


def greet(team, member, teams, members):
    barrier = pltpu.get_barrier_semaphore()
    for d, e in greeted(teams, members):
        pl.semaphore_signal(
            barrier,
            inc=1,
            device_id=(partner(team, d), partner(member, e)),
            device_id_type=MESH,
        )
    return barrier


def flow_base(
    start_ref, section_ref, velocity_ref, spread_ref, halo_x_ref, halo_y_ref, base_ref
):
    fields, rows_x, rows_y = section_ref.shape
    lanes = lax.broadcasted_iota(jnp.int32, (rows_x, rows_y), 1)
    subs = lax.broadcasted_iota(jnp.int32, (rows_x, rows_y), 0)
    half_u = 0.5 * velocity_ref[0]
    half_v = 0.5 * velocity_ref[1]
    low_x = halo_x_ref[0].astype(F32)
    high_x = halo_x_ref[1].astype(F32)
    low_y = halo_y_ref[0].astype(F32)
    high_y = halo_y_ref[1].astype(F32)
    for f in range(fields):
        here = section_ref[f]
        plus_x = jnp.where(
            subs == rows_x - 1, high_x[f : f + 1], pltpu.roll(here, rows_x - 1, 0)
        )
        minus_x = jnp.where(subs == 0, low_x[f : f + 1], pltpu.roll(here, 1, 0))
        plus_y = jnp.where(
            lanes == rows_y - 1,
            pltpu.roll(high_y, rows_y - 1 - f, 1),
            pltpu.roll(here, rows_y - 1, 1),
        )
        edge = pltpu.roll(low_y, (rows_y - f) % rows_y, 1) if f else low_y
        minus_y = jnp.where(lanes == 0, edge, pltpu.roll(here, 1, 1))
        flow = (
            spread_ref[f] * (plus_x + minus_x + plus_y + minus_y - 4.0 * here)
            - half_u * (plus_x - minus_x)
            - half_v * (plus_y - minus_y)
        )
        base_ref[f] = 0.75 * start_ref[f] + 0.25 * (here + TIME_STEP * flow)


def network_sum(states, w_in, w_mid, w_low, w_out, hidden_one, hidden_two, hidden_three):
    count = states.shape[1]

    def layer(weight, source, target):
        total = weight.shape[0]
        half = -(-total // 32) * 16
        for start in range(0, total, half):
            size = min(half, total - start)
            out = jnp.dot(weight[start : start + size, :], source, preferred_element_type=F32)
            target[start : start + size, :count] = silu(out).astype(BF16)

    layer(w_in, states, hidden_one)
    layer(w_mid.at[0, 0], hidden_one[:, :count], hidden_two)
    layer(w_low.at[0, 0], hidden_two[:, :count], hidden_three)
    return jnp.dot(w_out[0, 0], hidden_three[:, :count], preferred_element_type=F32)


def fused_kernel(
    teams,
    members,
    extra,
    section_hbm,
    start_hbm,
    velocity_hbm,
    cells_hbm,
    teams_hbm,
    spread_hbm,
    w_in_hbm,
    w_mid_hbm,
    w_low_hbm,
    w_out_hbm,
    own_ref,
    base_ref,
    flag_ref,
    section_ref,
    start_ref,
    velocity_ref,
    cells_ref,
    teams_ref,
    team_of,
    spread_ref,
    w_in_raw,
    w_in,
    w_mid,
    w_low,
    w_out,
    hidden_one,
    hidden_two,
    hidden_three,
    second,
    result,
    packed,
    back,
    chosen,
    got,
    edge_x,
    edge_y,
    halo_x,
    halo_y,
    rank_of,
    load_sem,
    send_b,
    recv_b,
    send_p,
    recv_p,
    send_r,
    recv_r,
    send_m,
    recv_m,
    send_h,
    recv_h,
    *rows,
):
    team = lax.axis_index("team")
    member = lax.axis_index("member")
    loads = []
    for k, (source, target) in enumerate(
        (
            (cells_hbm, cells_ref),
            (section_hbm, section_ref),
            (teams_hbm, team_of),
            (teams_hbm, teams_ref),
            (w_in_hbm, w_in_raw),
            (w_mid_hbm, w_mid),
            (w_low_hbm, w_low),
            (w_out_hbm, w_out),
            (spread_hbm, spread_ref),
            (velocity_hbm, velocity_ref),
            (start_hbm, start_ref),
        )
    ):
        copy = pltpu.make_async_copy(source, target, load_sem.at[k])
        if k < FIRST:
            copy.start()
        loads.append(copy)
    barrier = greet(team, member, teams, members)
    fields, rows_x, rows_y = section_ref.shape
    loads[0].wait()
    cells_x, cells_y = split_cells(cells_ref[...], rows_y)
    count = cells_x.shape[1]
    pick_y = (lax.broadcasted_iota(jnp.int32, (rows_y, count), 0) == cells_y).astype(F32)
    pick_x = row_mask(cells_x, rows_x)
    loads[1].wait()
    for copy in loads[FIRST:]:
        copy.start()
    flat = section_ref[...].reshape(fields * rows_x, rows_y).astype(BF16)
    taken = jnp.dot(flat, pick_y.astype(BF16), preferred_element_type=F32)
    taken = taken.reshape(fields, rows_x, count)
    own = jnp.sum(jnp.where(pick_x[None], taken, 0.0), axis=1)
    rows[0][member] = own.astype(BF16)
    pl.semaphore_wait(barrier, len(greeted(teams, members)))

    def remote(source, target, send, recv, device):
        copy = pltpu.make_async_remote_copy(
            src_ref=source,
            dst_ref=target,
            send_sem=send,
            recv_sem=recv,
            device_id=device,
            device_id_type=MESH,
        )
        copy.start()
        return copy

    direct = {}
    for d, e in straight(teams, members):
        direct[d, e] = remote(
            rows[0].at[member],
            rows[d].at[member],
            send_b.at[d, e],
            recv_b.at[d, e],
            (partner(team, d), partner(member, e)),
        )

    edge_x[0] = section_ref[:, rows_x - 1, :].astype(BF16)
    edge_x[1] = section_ref[:, 0, :].astype(BF16)
    loads[2].wait()
    picks = []
    found = jnp.int32(0)
    sources = [jnp.int32(0)] * extra
    for d in range(teams):
        base = partner(team, d) * members
        first = jnp.int32(0)
        later = jnp.int32(0)
        held = jnp.int32(0)
        for q in range(members - 1, -1, -1):
            here = team_of[0, base + q] == team
            later = jnp.where(here, first, later)
            first = jnp.where(here, q, first)
            held = held + here.astype(jnp.int32)
        picks.append((first, later))
        if extra < teams:
            twice = held > 1
            rank_of[d] = jnp.minimum(found, extra - 1)
            for k in range(extra):
                sources[k] = jnp.where(
                    jnp.logical_and(twice, found == k), jnp.int32(d), sources[k]
                )
            found = found + twice.astype(jnp.int32)
        else:
            rank_of[d] = jnp.int32(d)
            sources[d] = jnp.int32(d)
    loads[4].wait()
    w_in[...] = w_in_raw[0, 0].T
    lanes = lax.broadcasted_iota(jnp.int32, (rows_x, rows_y), 1)
    low = jnp.zeros((rows_x, rows_y), F32)
    high = jnp.zeros((rows_x, rows_y), F32)
    for f in range(fields):
        plane = section_ref[f]
        here = lanes == f
        high = jnp.where(here, pltpu.roll(plane, (f + 1) % rows_y, 1), high)
        low = jnp.where(here, pltpu.roll(plane, f, 1) if f else plane, low)
    edge_y[0] = high.astype(BF16)
    edge_y[1] = low.astype(BF16)
    halos = []
    for k, (step, edge, halo, along) in enumerate(
        (
            (1, edge_x.at[0], halo_x.at[0], "team"),
            (-1, edge_x.at[1], halo_x.at[1], "team"),
            (1, edge_y.at[0], halo_y.at[0], "member"),
            (-1, edge_y.at[1], halo_y.at[1], "member"),
        )
    ):
        if along == "team":
            device = (lax.rem(team + step + teams, teams), member)
        else:
            device = (team, lax.rem(member + step + members, members))
        halos.append(remote(edge, halo, send_h.at[k], recv_h.at[k], device))

    loads[3].wait()
    blocks_all = teams * members
    row = teams_ref[...]
    hits = (lax.broadcasted_iota(jnp.int32, (teams, blocks_all), 0) == row).astype(F32)
    ids = lax.broadcasted_iota(jnp.int32, (blocks_all, teams), 0)
    groups = lax.broadcasted_iota(jnp.int32, (blocks_all, teams), 1)
    inside = jnp.logical_and(ids >= groups * members, ids < (groups + 1) * members)
    tally = jnp.dot(hits.astype(BF16), inside.astype(F32).astype(BF16), preferred_element_type=F32)
    seconds_of = jnp.sum(jnp.where(tally > 1.5, 1.0, 0.0), axis=1, keepdims=True)
    most = jnp.max(seconds_of, axis=0, keepdims=True)
    flag_ref[...] = (most > extra + 0.5).astype(jnp.int32)

    for copy in loads[5:8]:
        copy.wait()
    nets = (w_in, w_mid, w_low, w_out, hidden_one, hidden_two, hidden_three)
    returns = []
    passed = {}

    def give(slot, d, target):
        returns.append(
            remote(
                result.at[slot, d],
                back.at[slot * teams + team],
                send_r.at[slot, d],
                recv_r.at[slot, d],
                (target, member),
            )
        )

    def arrive(d):
        if (d, 0) in direct or d == 0:
            for e in range(members):
                if d or e:
                    direct[d, e].wait_recv()
        else:
            passed[d].wait_recv()
        second[d] = rows[d][picks[d][1]]

    def primary(unit):
        states = jnp.concatenate([rows[d][picks[d][0]] for d in unit], axis=1)
        rates = network_sum(states, *nets)
        for k, d in enumerate(unit):
            piece = rates[:, k * count : (k + 1) * count]
            if d:
                result[0, d] = piece
                give(0, d, partner(team, d))
            else:
                back[team] = piece

    near = [d for d in range(min(2, teams))]
    for d in near:
        arrive(d)
    primary(near)
    evens = list(range(4, teams, 2))
    for d in evens + list(range(2, min(4, teams), 2)):
        arrive(d)
        passed[d + 1] = remote(
            rows[d], rows[d + 1], send_p.at[d], recv_p.at[d], (partner(team, 1), member)
        )
    for k in range(0, len(evens), 2):
        primary(evens[k : k + 2])
    for d in range(3, teams, 2):
        arrive(d)
    for start in range(0, extra, GROUP):
        spots = range(start, min(start + GROUP, extra))
        states = jnp.concatenate([second[sources[k]] for k in spots], axis=1)
        rates = network_sum(states, *nets)
        for k, spot in enumerate(spots):
            packed[spot] = rates[:, k * count : (k + 1) * count]
    for d in range(1, teams):
        result[1, d] = packed[rank_of[d]]
        give(1, d, partner(team, d))
    back[teams + team] = packed[rank_of[0]]
    odds = list(range(5, teams, 2))
    for k in range(0, len(odds), 2):
        primary(odds[k : k + 2])
    if teams > 2:
        primary([2, 3])

    for copy in loads[8:]:
        copy.wait()
    for copy in halos:
        copy.wait_recv()
    flow_base(start_ref, section_ref, velocity_ref, spread_ref, halo_x, halo_y, base_ref)
    where = []
    for q in range(members):
        regime = team_of[0, team * members + q]
        rank = jnp.int32(0)
        for other in range(q):
            rank = rank + (team_of[0, team * members + other] == regime).astype(jnp.int32)
        where.append(jnp.minimum(rank, CAP - 1) * teams + regime)
    for copy in returns:
        copy.wait_recv()
    for q in range(members):
        chosen[q] = back[where[q]]
    sends = []
    for e in range(members - 1, 0, -1):
        target = partner(member, e)
        sends.append(
            remote(chosen.at[target], got.at[e], send_m.at[e], recv_m.at[e], (team, target))
        )
    total = chosen[member]
    for e in range(1, members):
        sends[members - 1 - e].wait_recv()
        total = total + got[e]
    own_ref[...] = total
    for copy in list(direct.values()) + list(passed.values()) + halos + returns + sends:
        copy.wait_send()


def update_kernel(
    groups, cells_ref, rates_ref, base_ref, source_out, new_out, source_ref, new_ref, sems
):
    fields, rows_x, rows_y = base_ref.shape
    cells_x, cells_y = split_cells(cells_ref[...], rows_y)
    count = cells_x.shape[1]
    pick_x = row_mask(cells_x, rows_x)
    pick_y = (lax.broadcasted_iota(jnp.int32, (rows_y, count), 0) == cells_y).astype(F32)
    pick_y = pick_y.astype(BF16)
    pick_y = jnp.concatenate([pick_y, pick_y], axis=1)
    group = fields // groups
    copies = []
    for f in range(fields):
        spread_rates = jnp.where(pick_x, rates_ref[f : f + 1, :], 0.0)
        top = spread_rates.astype(BF16)
        rest = (spread_rates - top.astype(F32)).astype(BF16)
        source = lax.dot_general(
            jnp.concatenate([top, rest], axis=1),
            pick_y,
            (((1,), (1,)), ((), ())),
            preferred_element_type=F32,
        )
        source_ref[f] = source
        new_ref[f] = base_ref[f] + (0.25 * TIME_STEP) * source
        if (f + 1) % group == 0:
            span = pl.ds(f + 1 - group, group)
            for k, (held, out) in enumerate(((source_ref, source_out), (new_ref, new_out))):
                copy = pltpu.make_async_copy(held.at[span], out.at[span], sems.at[k, f // group])
                copy.start()
                copies.append(copy)
    for copy in copies:
        copy.wait()


def whole(space=VMEM):
    return pl.BlockSpec(memory_space=space)


def shards(
    state_start,
    state_section,
    velocity,
    diffusivity,
    flame_cells,
    block_team,
    w_in,
    w_mid,
    w_low,
    w_out,
):
    teams = lax.axis_size("team")
    members = lax.axis_size("member")
    fields, rows_x, rows_y = state_section.shape
    count = flame_cells.shape[1]
    dma = pltpu.SemaphoreType.DMA
    w_in = jnp.swapaxes(w_in, 2, 3)
    hidden = w_in.shape[3]
    wide = min(GROUP, teams) * count
    operands = (
        state_section,
        state_start,
        velocity,
        flame_cells,
        block_team.reshape(1, -1),
        diffusivity,
        w_in,
        w_mid,
        w_low,
        w_out,
    )

    def networks(extra, collective, name, operands):
        return pl.pallas_call(
            functools.partial(fused_kernel, teams, members, extra),
            out_shape=(
                jax.ShapeDtypeStruct((fields, count), F32),
                jax.ShapeDtypeStruct(state_section.shape, F32),
                jax.ShapeDtypeStruct((1, 1), jnp.int32),
            ),
            in_specs=[whole(pltpu.HBM)] * len(operands),
            out_specs=(whole(), whole(), whole()),
            scratch_shapes=[
                VMEM(state_section.shape, F32),
                VMEM(state_start.shape, F32),
                VMEM(velocity.shape, F32),
                VMEM(flame_cells.shape, jnp.int32),
                VMEM((1, teams * members), jnp.int32),
                pltpu.SMEM((1, teams * members), jnp.int32),
                pltpu.SMEM(diffusivity.shape, F32),
                VMEM(w_in.shape, BF16),
                VMEM((hidden, fields), BF16),
                VMEM(w_mid.shape, BF16),
                VMEM(w_low.shape, BF16),
                VMEM(w_out.shape, BF16),
                VMEM((hidden, wide), BF16),
                VMEM((w_mid.shape[2], wide), BF16),
                VMEM((w_low.shape[2], wide), BF16),
                VMEM((teams, fields, count), BF16),
                VMEM((CAP, teams, fields, count), F32),
                VMEM((extra, fields, count), F32),
                VMEM((CAP * teams, fields, count), F32),
                VMEM((members, fields, count), F32),
                VMEM((members, fields, count), F32),
                VMEM((2, fields, rows_y), BF16),
                VMEM((2, rows_x, rows_y), BF16),
                VMEM((2, fields, rows_y), BF16),
                VMEM((2, rows_x, rows_y), BF16),
                pltpu.SMEM((teams,), jnp.int32),
                dma((11,)),
                dma((teams, members)),
                dma((teams, members)),
                dma((teams,)),
                dma((teams,)),
                dma((CAP, teams)),
                dma((CAP, teams)),
                dma((members,)),
                dma((members,)),
                dma((4,)),
                dma((4,)),
            ]
            + [VMEM((members, fields, count), BF16)] * teams,
            compiler_params=pltpu.CompilerParams(
                collective_id=collective, has_side_effects=True, vmem_limit_bytes=GRANT
            ),
            name=name,
        )(*[pltpu.with_memory_space_constraint(x, pltpu.HBM) for x in operands])

    extra = max(2, teams // 4)
    rates, base, full = networks(extra, 0, "networks", operands)
    rates = lax.cond(
        full[0, 0] == 0,
        lambda rates, *operands: rates,
        lambda rates, *operands: networks(teams, 1, "general", operands)[0],
        rates,
        *operands,
    )
    groups = 6 if fields % 6 == 0 else fields
    return pl.pallas_call(
        functools.partial(update_kernel, groups),
        out_shape=(
            jax.ShapeDtypeStruct(state_section.shape, F32),
            jax.ShapeDtypeStruct(state_section.shape, F32),
        ),
        in_specs=[whole()] * 3,
        out_specs=(whole(pl.ANY), whole(pl.ANY)),
        scratch_shapes=[
            VMEM(state_section.shape, F32),
            VMEM(state_section.shape, F32),
            dma((2, groups)),
        ],
        compiler_params=pltpu.CompilerParams(vmem_limit_bytes=GRANT),
        name="update",
    )(flame_cells, rates, base)


def solution(mesh):
    grid = P(None, "team", "member")
    weights = P("team", "member", None, None)
    placed = (
        grid,
        grid,
        grid,
        P(),
        P(("team", "member"), None),
        P(),
        weights,
        weights,
        weights,
        weights,
    )
    return jax.shard_map(
        shards, mesh=mesh, in_specs=placed, out_specs=(grid, grid), check_vma=False
    )
```

```python
import functools

import jax
import jax.numpy as jnp
from jax import lax
from jax.experimental import pallas as pl
from jax.experimental.pallas import tpu as pltpu
from jax.sharding import PartitionSpec as P

CAP = 2
TIME_STEP = 0.25
GRANT = 24 << 20
GROUP = 4
FIRST = 4
MESH = pl.DeviceIdType.MESH
VMEM = pltpu.VMEM
F32 = jnp.float32
BF16 = jnp.bfloat16


def partner(index, flips):
    target = index
    bit = 1
    while bit <= flips:
        if flips & bit:
            target = target + bit - 2 * bit * lax.rem(index // bit, 2)
        bit *= 2
    return target


def split_cells(cells, rows_y):
    shift = rows_y.bit_length() - 1
    assert rows_y == 1 << shift
    return cells >> shift, cells & (rows_y - 1)


def row_mask(cells_x, rows_x):
    count = cells_x.shape[1]
    return lax.broadcasted_iota(jnp.int32, (rows_x, count), 0) == cells_x


def silu(x):
    half = 0.5 * x
    return half + half * jnp.tanh(half)


def straight(teams, members):
    order = [(d, e) for d in range(4, teams, 2) for e in range(members)]
    order += [(0, e) for e in range(1, members)]
    order += [(1, e) for e in range(members)] if teams > 1 else []
    order += [(2, e) for e in range(members)] if teams > 2 else []
    return order


def greeted(teams, members):
    order = straight(teams, members)
    return order + [(d, 0) for d in range(1, teams) if (d, 0) not in order]


def greet(team, member, teams, members):
    barrier = pltpu.get_barrier_semaphore()
    for d, e in greeted(teams, members):
        pl.semaphore_signal(
            barrier,
            inc=1,
            device_id=(partner(team, d), partner(member, e)),
            device_id_type=MESH,
        )
    return barrier


def flow_base(
    start_ref, section_ref, velocity_ref, spread_ref, halo_x_ref, halo_y_ref, base_ref
):
    fields, rows_x, rows_y = section_ref.shape
    lanes = lax.broadcasted_iota(jnp.int32, (rows_x, rows_y), 1)
    subs = lax.broadcasted_iota(jnp.int32, (rows_x, rows_y), 0)
    half_u = 0.5 * velocity_ref[0]
    half_v = 0.5 * velocity_ref[1]
    low_x = halo_x_ref[0].astype(F32)
    high_x = halo_x_ref[1].astype(F32)
    low_y = halo_y_ref[0].astype(F32)
    high_y = halo_y_ref[1].astype(F32)
    for f in range(fields):
        here = section_ref[f]
        plus_x = jnp.where(
            subs == rows_x - 1, high_x[f : f + 1], pltpu.roll(here, rows_x - 1, 0)
        )
        minus_x = jnp.where(subs == 0, low_x[f : f + 1], pltpu.roll(here, 1, 0))
        plus_y = jnp.where(
            lanes == rows_y - 1,
            pltpu.roll(high_y, rows_y - 1 - f, 1),
            pltpu.roll(here, rows_y - 1, 1),
        )
        edge = pltpu.roll(low_y, (rows_y - f) % rows_y, 1) if f else low_y
        minus_y = jnp.where(lanes == 0, edge, pltpu.roll(here, 1, 1))
        flow = (
            spread_ref[f] * (plus_x + minus_x + plus_y + minus_y - 4.0 * here)
            - half_u * (plus_x - minus_x)
            - half_v * (plus_y - minus_y)
        )
        base_ref[f] = 0.75 * start_ref[f] + 0.25 * (here + TIME_STEP * flow)


def network_sum(states, w_in, w_mid, w_low, w_out, hidden_one, hidden_two, hidden_three):
    count = states.shape[1]

    def layer(weight, source, target):
        total = weight.shape[0]
        half = -(-total // 32) * 16
        for start in range(0, total, half):
            size = min(half, total - start)
            out = jnp.dot(weight[start : start + size, :], source, preferred_element_type=F32)
            target[start : start + size, :count] = silu(out).astype(BF16)

    layer(w_in, states, hidden_one)
    layer(w_mid.at[0, 0], hidden_one[:, :count], hidden_two)
    layer(w_low.at[0, 0], hidden_two[:, :count], hidden_three)
    return jnp.dot(w_out[0, 0], hidden_three[:, :count], preferred_element_type=F32)


def fused_kernel(
    teams,
    members,
    extra,
    section_hbm,
    start_hbm,
    velocity_hbm,
    cells_hbm,
    teams_hbm,
    spread_hbm,
    w_in_hbm,
    w_mid_hbm,
    w_low_hbm,
    w_out_hbm,
    own_ref,
    base_ref,
    flag_ref,
    section_ref,
    start_ref,
    velocity_ref,
    cells_ref,
    teams_ref,
    team_of,
    spread_ref,
    w_in_raw,
    w_in,
    w_mid,
    w_low,
    w_out,
    hidden_one,
    hidden_two,
    hidden_three,
    second,
    result,
    packed,
    back,
    chosen,
    got,
    edge_x,
    edge_y,
    halo_x,
    halo_y,
    rank_of,
    load_sem,
    send_b,
    recv_b,
    send_p,
    recv_p,
    send_r,
    recv_r,
    send_m,
    recv_m,
    send_h,
    recv_h,
    *rows,
):
    team = lax.axis_index("team")
    member = lax.axis_index("member")
    loads = []
    for k, (source, target) in enumerate(
        (
            (cells_hbm, cells_ref),
            (section_hbm, section_ref),
            (teams_hbm, team_of),
            (teams_hbm, teams_ref),
            (w_in_hbm, w_in_raw),
            (w_mid_hbm, w_mid),
            (w_low_hbm, w_low),
            (w_out_hbm, w_out),
            (spread_hbm, spread_ref),
            (velocity_hbm, velocity_ref),
            (start_hbm, start_ref),
        )
    ):
        copy = pltpu.make_async_copy(source, target, load_sem.at[k])
        if k < FIRST:
            copy.start()
        loads.append(copy)
    barrier = greet(team, member, teams, members)
    fields, rows_x, rows_y = section_ref.shape
    loads[0].wait()
    cells_x, cells_y = split_cells(cells_ref[...], rows_y)
    count = cells_x.shape[1]
    pick_y = (lax.broadcasted_iota(jnp.int32, (rows_y, count), 0) == cells_y).astype(F32)
    pick_x = row_mask(cells_x, rows_x)
    loads[1].wait()
    for copy in loads[FIRST:]:
        copy.start()
    flat = section_ref[...].reshape(fields * rows_x, rows_y).astype(BF16)
    taken = jnp.dot(flat, pick_y.astype(BF16), preferred_element_type=F32)
    taken = taken.reshape(fields, rows_x, count)
    own = jnp.sum(jnp.where(pick_x[None], taken, 0.0), axis=1)
    rows[0][member] = own.astype(BF16)
    pl.semaphore_wait(barrier, len(greeted(teams, members)))

    def bytes_of(ref, semaphore):
        pltpu.make_async_copy(ref, ref, semaphore).wait()

    def remote(source, target, send, recv, device):
        copy = pltpu.make_async_remote_copy(
            src_ref=source,
            dst_ref=target,
            send_sem=send,
            recv_sem=recv,
            device_id=device,
            device_id_type=MESH,
        )
        copy.start()
        return copy

    direct = {}
    heads = sorted({d for d, _ in straight(teams, members)})
    place = {d: k for k, d in enumerate(heads)}
    for d, e in straight(teams, members):
        direct[d, e] = remote(
            rows[0].at[member],
            rows[d].at[member],
            send_b.at[place[d]],
            recv_b.at[place[d]],
            (partner(team, d), partner(member, e)),
        )

    edge_x[0] = section_ref[:, rows_x - 1, :].astype(BF16)
    edge_x[1] = section_ref[:, 0, :].astype(BF16)
    loads[2].wait()
    picks = []
    found = jnp.int32(0)
    sources = [jnp.int32(0)] * extra
    for d in range(teams):
        base = partner(team, d) * members
        first = jnp.int32(0)
        later = jnp.int32(0)
        held = jnp.int32(0)
        for q in range(members - 1, -1, -1):
            here = team_of[0, base + q] == team
            later = jnp.where(here, first, later)
            first = jnp.where(here, q, first)
            held = held + here.astype(jnp.int32)
        picks.append((first, later))
        if extra < teams:
            twice = held > 1
            rank_of[d] = jnp.minimum(found, extra - 1)
            for k in range(extra):
                sources[k] = jnp.where(
                    jnp.logical_and(twice, found == k), jnp.int32(d), sources[k]
                )
            found = found + twice.astype(jnp.int32)
        else:
            rank_of[d] = jnp.int32(d)
            sources[d] = jnp.int32(d)
    loads[4].wait()
    w_in[...] = w_in_raw[0, 0].T
    lanes = lax.broadcasted_iota(jnp.int32, (rows_x, rows_y), 1)
    low = jnp.zeros((rows_x, rows_y), F32)
    high = jnp.zeros((rows_x, rows_y), F32)
    for f in range(fields):
        plane = section_ref[f]
        here = lanes == f
        high = jnp.where(here, pltpu.roll(plane, (f + 1) % rows_y, 1), high)
        low = jnp.where(here, pltpu.roll(plane, f, 1) if f else plane, low)
    edge_y[0] = high.astype(BF16)
    edge_y[1] = low.astype(BF16)
    for k, (step, edge, halo, along) in enumerate(
        (
            (1, edge_x.at[0], halo_x.at[0], "team"),
            (-1, edge_x.at[1], halo_x.at[1], "team"),
            (1, edge_y.at[0], halo_y.at[0], "member"),
            (-1, edge_y.at[1], halo_y.at[1], "member"),
        )
    ):
        if along == "team":
            device = (lax.rem(team + step + teams, teams), member)
        else:
            device = (team, lax.rem(member + step + members, members))
        remote(edge, halo, send_h.at[k // 2], recv_h.at[k // 2], device)

    loads[3].wait()
    blocks_all = teams * members
    row = teams_ref[...]
    hits = (lax.broadcasted_iota(jnp.int32, (teams, blocks_all), 0) == row).astype(F32)
    ids = lax.broadcasted_iota(jnp.int32, (blocks_all, teams), 0)
    groups = lax.broadcasted_iota(jnp.int32, (blocks_all, teams), 1)
    inside = jnp.logical_and(ids >= groups * members, ids < (groups + 1) * members)
    tally = jnp.dot(hits.astype(BF16), inside.astype(F32).astype(BF16), preferred_element_type=F32)
    seconds_of = jnp.sum(jnp.where(tally > 1.5, 1.0, 0.0), axis=1, keepdims=True)
    most = jnp.max(seconds_of, axis=0, keepdims=True)
    flag_ref[...] = (most > extra + 0.5).astype(jnp.int32)

    for copy in loads[5:8]:
        copy.wait()
    nets = (w_in, w_mid, w_low, w_out, hidden_one, hidden_two, hidden_three)
    passed = {}

    def give(slot, d, target):
        remote(
            result.at[slot * (teams - 1) + d - 1],
            back.at[slot * teams + team],
            send_r,
            recv_r,
            (target, member),
        )

    def arrive(d):
        if d in place:
            held = rows[d] if d else rows[d].at[pl.ds(0, members - 1)]
            bytes_of(held, recv_b.at[place[d]])
        else:
            passed[d].wait_recv()
        second[d] = rows[d][picks[d][1]]

    def primary(unit):
        states = jnp.concatenate([rows[d][picks[d][0]] for d in unit], axis=1)
        rates = network_sum(states, *nets)
        for k, d in enumerate(unit):
            piece = rates[:, k * count : (k + 1) * count]
            if d:
                result[d - 1] = piece
                give(0, d, partner(team, d))
            else:
                back[team] = piece

    near = [d for d in range(min(2, teams))]
    for d in near:
        arrive(d)
    primary(near)
    evens = list(range(4, teams, 2))
    for d in evens + list(range(2, min(4, teams), 2)):
        arrive(d)
        passed[d + 1] = remote(
            rows[d], rows[d + 1], send_p.at[d // 2], recv_p.at[d // 2], (partner(team, 1), member)
        )
    for k in range(0, len(evens), 2):
        primary(evens[k : k + 2])
    for d in range(3, teams, 2):
        arrive(d)
    for start in range(0, extra, GROUP):
        spots = range(start, min(start + GROUP, extra))
        states = jnp.concatenate([second[sources[k]] for k in spots], axis=1)
        rates = network_sum(states, *nets)
        for k, spot in enumerate(spots):
            packed[spot] = rates[:, k * count : (k + 1) * count]
    for d in range(1, teams):
        result[teams + d - 2] = packed[rank_of[d]]
        give(1, d, partner(team, d))
    back[teams + team] = packed[rank_of[0]]
    odds = list(range(5, teams, 2))
    for k in range(0, len(odds), 2):
        primary(odds[k : k + 2])
    if teams > 2:
        primary([2, 3])

    for copy in loads[8:]:
        copy.wait()
    bytes_of(halo_x, recv_h.at[0])
    bytes_of(halo_y, recv_h.at[1])
    flow_base(start_ref, section_ref, velocity_ref, spread_ref, halo_x, halo_y, base_ref)
    where = []
    for q in range(members):
        regime = team_of[0, team * members + q]
        rank = jnp.int32(0)
        for other in range(q):
            rank = rank + (team_of[0, team * members + other] == regime).astype(jnp.int32)
        where.append(jnp.minimum(rank, CAP - 1) * teams + regime)
    bytes_of(back.at[pl.ds(0, CAP * (teams - 1))], recv_r)
    for q in range(members):
        chosen[q] = back[where[q]]
    for e in range(members - 1, 0, -1):
        target = partner(member, e)
        remote(chosen.at[target], got.at[e - 1], send_m, recv_m, (team, target))
    total = chosen[member]
    bytes_of(got, recv_m)
    for e in range(members - 1):
        total = total + got[e]
    own_ref[...] = total
    for d in heads:
        bytes_of(rows[d] if d else rows[d].at[pl.ds(0, members - 1)], send_b.at[place[d]])
    for copy in passed.values():
        copy.wait_send()
    bytes_of(edge_x, send_h.at[0])
    bytes_of(edge_y, send_h.at[1])
    bytes_of(result, send_r)
    bytes_of(got, send_m)


def update_kernel(
    groups, cells_ref, rates_ref, base_ref, source_out, new_out, source_ref, new_ref, sems
):
    fields, rows_x, rows_y = base_ref.shape
    cells_x, cells_y = split_cells(cells_ref[...], rows_y)
    count = cells_x.shape[1]
    pick_x = row_mask(cells_x, rows_x)
    pick_y = (lax.broadcasted_iota(jnp.int32, (rows_y, count), 0) == cells_y).astype(F32)
    pick_y = pick_y.astype(BF16)
    pick_y = jnp.concatenate([pick_y, pick_y], axis=1)
    group = fields // groups
    copies = []
    for f in range(fields):
        spread_rates = jnp.where(pick_x, rates_ref[f : f + 1, :], 0.0)
        top = spread_rates.astype(BF16)
        rest = (spread_rates - top.astype(F32)).astype(BF16)
        source = lax.dot_general(
            jnp.concatenate([top, rest], axis=1),
            pick_y,
            (((1,), (1,)), ((), ())),
            preferred_element_type=F32,
        )
        source_ref[f] = source
        new_ref[f] = base_ref[f] + (0.25 * TIME_STEP) * source
        if (f + 1) % group == 0:
            span = pl.ds(f + 1 - group, group)
            for k, (held, out) in enumerate(((source_ref, source_out), (new_ref, new_out))):
                copy = pltpu.make_async_copy(held.at[span], out.at[span], sems.at[k, f // group])
                copy.start()
                copies.append(copy)
    for copy in copies:
        copy.wait()


def whole(space=VMEM):
    return pl.BlockSpec(memory_space=space)


def shards(
    state_start,
    state_section,
    velocity,
    diffusivity,
    flame_cells,
    block_team,
    w_in,
    w_mid,
    w_low,
    w_out,
):
    teams = lax.axis_size("team")
    members = lax.axis_size("member")
    fields, rows_x, rows_y = state_section.shape
    count = flame_cells.shape[1]
    dma = pltpu.SemaphoreType.DMA
    w_in = jnp.swapaxes(w_in, 2, 3)
    hidden = w_in.shape[3]
    wide = min(GROUP, teams) * count
    heads = len({d for d, _ in straight(teams, members)})
    operands = (
        state_section,
        state_start,
        velocity,
        flame_cells,
        block_team.reshape(1, -1),
        diffusivity,
        w_in,
        w_mid,
        w_low,
        w_out,
    )

    def networks(extra, collective, name, operands):
        return pl.pallas_call(
            functools.partial(fused_kernel, teams, members, extra),
            out_shape=(
                jax.ShapeDtypeStruct((fields, count), F32),
                jax.ShapeDtypeStruct(state_section.shape, F32),
                jax.ShapeDtypeStruct((1, 1), jnp.int32),
            ),
            in_specs=[whole(pltpu.HBM)] * len(operands),
            out_specs=(whole(), whole(), whole()),
            scratch_shapes=[
                VMEM(state_section.shape, F32),
                VMEM(state_start.shape, F32),
                VMEM(velocity.shape, F32),
                VMEM(flame_cells.shape, jnp.int32),
                VMEM((1, teams * members), jnp.int32),
                pltpu.SMEM((1, teams * members), jnp.int32),
                pltpu.SMEM(diffusivity.shape, F32),
                VMEM(w_in.shape, BF16),
                VMEM((hidden, fields), BF16),
                VMEM(w_mid.shape, BF16),
                VMEM(w_low.shape, BF16),
                VMEM(w_out.shape, BF16),
                VMEM((hidden, wide), BF16),
                VMEM((w_mid.shape[2], wide), BF16),
                VMEM((w_low.shape[2], wide), BF16),
                VMEM((teams, fields, count), BF16),
                VMEM((CAP * (teams - 1), fields, count), F32),
                VMEM((extra, fields, count), F32),
                VMEM((CAP * teams, fields, count), F32),
                VMEM((members, fields, count), F32),
                VMEM((members - 1, fields, count), F32),
                VMEM((2, fields, rows_y), BF16),
                VMEM((2, rows_x, rows_y), BF16),
                VMEM((2, fields, rows_y), BF16),
                VMEM((2, rows_x, rows_y), BF16),
                pltpu.SMEM((teams,), jnp.int32),
                dma((11,)),
                dma((heads,)),
                dma((heads,)),
                dma((-(-teams // 2),)),
                dma((-(-teams // 2),)),
                dma,
                dma,
                dma,
                dma,
                dma((2,)),
                dma((2,)),
            ]
            + [VMEM((members, fields, count), BF16)] * teams,
            compiler_params=pltpu.CompilerParams(
                collective_id=collective, has_side_effects=True, vmem_limit_bytes=GRANT
            ),
            name=name,
        )(*[pltpu.with_memory_space_constraint(x, pltpu.HBM) for x in operands])

    extra = max(2, teams // 4)
    rates, base, full = networks(extra, 0, "networks", operands)
    rates = lax.cond(
        full[0, 0] == 0,
        lambda rates, *operands: rates,
        lambda rates, *operands: networks(teams, 1, "general", operands)[0],
        rates,
        *operands,
    )
    groups = 6 if fields % 6 == 0 else fields
    return pl.pallas_call(
        functools.partial(update_kernel, groups),
        out_shape=(
            jax.ShapeDtypeStruct(state_section.shape, F32),
            jax.ShapeDtypeStruct(state_section.shape, F32),
        ),
        in_specs=[whole()] * 3,
        out_specs=(whole(pl.ANY), whole(pl.ANY)),
        scratch_shapes=[
            VMEM(state_section.shape, F32),
            VMEM(state_section.shape, F32),
            dma((2, groups)),
        ],
        compiler_params=pltpu.CompilerParams(vmem_limit_bytes=GRANT),
        name="update",
    )(flame_cells, rates, base)


def solution(mesh):
    grid = P(None, "team", "member")
    weights = P("team", "member", None, None)
    placed = (
        grid,
        grid,
        grid,
        P(),
        P(("team", "member"), None),
        P(),
        weights,
        weights,
        weights,
        weights,
    )
    return jax.shard_map(
        shards, mesh=mesh, in_specs=placed, out_specs=(grid, grid), check_vma=False
    )
```

```python
import functools

import jax
import jax.numpy as jnp
from jax import lax
from jax.experimental import pallas as pl
from jax.experimental.pallas import tpu as pltpu
from jax.sharding import PartitionSpec as P

CAP = 2
TIME_STEP = 0.25
GRANT = 24 << 20
GROUP = 4
FIRST = 4
MESH = pl.DeviceIdType.MESH
VMEM = pltpu.VMEM
F32 = jnp.float32
BF16 = jnp.bfloat16


def partner(index, flips):
    target = index
    bit = 1
    while bit <= flips:
        if flips & bit:
            target = target + bit - 2 * bit * lax.rem(index // bit, 2)
        bit *= 2
    return target


def split_cells(cells, rows_y):
    shift = rows_y.bit_length() - 1
    assert rows_y == 1 << shift
    return cells >> shift, cells & (rows_y - 1)


def row_mask(cells_x, rows_x):
    count = cells_x.shape[1]
    return lax.broadcasted_iota(jnp.int32, (rows_x, count), 0) == cells_x


def silu(x):
    half = 0.5 * x
    return half + half * jnp.tanh(half)


def straight(teams, members):
    order = [(0, e) for e in range(1, members)]
    order += [(1, e) for e in range(members)] if teams > 1 else []
    order += [(d, e) for d in range(4, teams, 2) for e in range(members)]
    order += [(2, e) for e in range(members)] if teams > 2 else []
    return order


def greeted(teams, members):
    order = straight(teams, members)
    return order + [(d, 0) for d in range(1, teams) if (d, 0) not in order]


def greet(team, member, teams, members):
    barrier = pltpu.get_barrier_semaphore()
    for d, e in greeted(teams, members):
        pl.semaphore_signal(
            barrier,
            inc=1,
            device_id=(partner(team, d), partner(member, e)),
            device_id_type=MESH,
        )
    return barrier


def flow_base(
    start_ref, section_ref, velocity_ref, spread_ref, halo_x_ref, halo_y_ref, base_ref
):
    fields, rows_x, rows_y = section_ref.shape
    lanes = lax.broadcasted_iota(jnp.int32, (rows_x, rows_y), 1)
    subs = lax.broadcasted_iota(jnp.int32, (rows_x, rows_y), 0)
    half_u = 0.5 * velocity_ref[0]
    half_v = 0.5 * velocity_ref[1]
    low_x = halo_x_ref[0].astype(F32)
    high_x = halo_x_ref[1].astype(F32)
    low_y = halo_y_ref[0].astype(F32)
    high_y = halo_y_ref[1].astype(F32)
    for f in range(fields):
        here = section_ref[f]
        plus_x = jnp.where(
            subs == rows_x - 1, high_x[f : f + 1], pltpu.roll(here, rows_x - 1, 0)
        )
        minus_x = jnp.where(subs == 0, low_x[f : f + 1], pltpu.roll(here, 1, 0))
        plus_y = jnp.where(
            lanes == rows_y - 1,
            pltpu.roll(high_y, rows_y - 1 - f, 1),
            pltpu.roll(here, rows_y - 1, 1),
        )
        edge = pltpu.roll(low_y, (rows_y - f) % rows_y, 1) if f else low_y
        minus_y = jnp.where(lanes == 0, edge, pltpu.roll(here, 1, 1))
        flow = (
            spread_ref[f] * (plus_x + minus_x + plus_y + minus_y - 4.0 * here)
            - half_u * (plus_x - minus_x)
            - half_v * (plus_y - minus_y)
        )
        base_ref[f] = 0.75 * start_ref[f] + 0.25 * (here + TIME_STEP * flow)


def network_sum(states, w_in, w_mid, w_low, w_out, hidden_one, hidden_two, hidden_three):
    count = states.shape[1]

    def layer(weight, source, target):
        total = weight.shape[0]
        half = -(-total // 32) * 16
        for start in range(0, total, half):
            size = min(half, total - start)
            out = jnp.dot(weight[start : start + size, :], source, preferred_element_type=F32)
            target[start : start + size, :count] = silu(out).astype(BF16)

    layer(w_in, states, hidden_one)
    layer(w_mid.at[0, 0], hidden_one[:, :count], hidden_two)
    layer(w_low.at[0, 0], hidden_two[:, :count], hidden_three)
    return jnp.dot(w_out[0, 0], hidden_three[:, :count], preferred_element_type=F32)


def fused_kernel(
    teams,
    members,
    extra,
    section_hbm,
    start_hbm,
    velocity_hbm,
    cells_hbm,
    teams_hbm,
    spread_hbm,
    w_in_hbm,
    w_mid_hbm,
    w_low_hbm,
    w_out_hbm,
    own_ref,
    base_ref,
    flag_ref,
    section_ref,
    start_ref,
    velocity_ref,
    cells_ref,
    teams_ref,
    team_of,
    spread_ref,
    w_in_raw,
    w_in,
    w_mid,
    w_low,
    w_out,
    hidden_one,
    hidden_two,
    hidden_three,
    second,
    result,
    packed,
    back,
    chosen,
    got,
    edge_x,
    edge_y,
    halo_x,
    halo_y,
    rank_of,
    load_sem,
    send_b,
    recv_b,
    send_p,
    recv_p,
    send_r,
    recv_r,
    send_m,
    recv_m,
    send_h,
    recv_h,
    *rows,
):
    team = lax.axis_index("team")
    member = lax.axis_index("member")
    loads = []
    for k, (source, target) in enumerate(
        (
            (cells_hbm, cells_ref),
            (section_hbm, section_ref),
            (teams_hbm, team_of),
            (teams_hbm, teams_ref),
            (w_in_hbm, w_in_raw),
            (w_mid_hbm, w_mid),
            (w_low_hbm, w_low),
            (w_out_hbm, w_out),
            (spread_hbm, spread_ref),
            (velocity_hbm, velocity_ref),
            (start_hbm, start_ref),
        )
    ):
        copy = pltpu.make_async_copy(source, target, load_sem.at[k])
        if k < FIRST:
            copy.start()
        loads.append(copy)
    barrier = greet(team, member, teams, members)
    fields, rows_x, rows_y = section_ref.shape
    loads[0].wait()
    cells_x, cells_y = split_cells(cells_ref[...], rows_y)
    count = cells_x.shape[1]
    pick_y = (lax.broadcasted_iota(jnp.int32, (rows_y, count), 0) == cells_y).astype(F32)
    pick_x = row_mask(cells_x, rows_x)
    loads[1].wait()
    for copy in loads[FIRST:]:
        copy.start()
    flat = section_ref[...].reshape(fields * rows_x, rows_y).astype(BF16)
    taken = jnp.dot(flat, pick_y.astype(BF16), preferred_element_type=F32)
    taken = taken.reshape(fields, rows_x, count)
    own = jnp.sum(jnp.where(pick_x[None], taken, 0.0), axis=1)
    rows[0][member] = own.astype(BF16)
    pl.semaphore_wait(barrier, len(greeted(teams, members)))

    def bytes_of(ref, semaphore):
        pltpu.make_async_copy(ref, ref, semaphore).wait()

    def remote(source, target, send, recv, device):
        copy = pltpu.make_async_remote_copy(
            src_ref=source,
            dst_ref=target,
            send_sem=send,
            recv_sem=recv,
            device_id=device,
            device_id_type=MESH,
        )
        copy.start()
        return copy

    direct = {}
    heads = sorted({d for d, _ in straight(teams, members)})
    place = {d: k for k, d in enumerate(heads)}
    for d, e in straight(teams, members):
        direct[d, e] = remote(
            rows[0].at[member],
            rows[d].at[member],
            send_b.at[place[d]],
            recv_b.at[place[d]],
            (partner(team, d), partner(member, e)),
        )

    edge_x[0] = section_ref[:, rows_x - 1, :].astype(BF16)
    edge_x[1] = section_ref[:, 0, :].astype(BF16)
    loads[2].wait()
    picks = []
    found = jnp.int32(0)
    sources = [jnp.int32(0)] * extra
    for d in range(teams):
        base = partner(team, d) * members
        first = jnp.int32(0)
        later = jnp.int32(0)
        held = jnp.int32(0)
        for q in range(members - 1, -1, -1):
            here = team_of[0, base + q] == team
            later = jnp.where(here, first, later)
            first = jnp.where(here, q, first)
            held = held + here.astype(jnp.int32)
        picks.append((first, later))
        if extra < teams:
            twice = held > 1
            rank_of[d] = jnp.minimum(found, extra - 1)
            for k in range(extra):
                sources[k] = jnp.where(
                    jnp.logical_and(twice, found == k), jnp.int32(d), sources[k]
                )
            found = found + twice.astype(jnp.int32)
        else:
            rank_of[d] = jnp.int32(d)
            sources[d] = jnp.int32(d)
    loads[4].wait()
    w_in[...] = w_in_raw[0, 0].T
    lanes = lax.broadcasted_iota(jnp.int32, (rows_x, rows_y), 1)
    low = jnp.zeros((rows_x, rows_y), F32)
    high = jnp.zeros((rows_x, rows_y), F32)
    for f in range(fields):
        plane = section_ref[f]
        here = lanes == f
        high = jnp.where(here, pltpu.roll(plane, (f + 1) % rows_y, 1), high)
        low = jnp.where(here, pltpu.roll(plane, f, 1) if f else plane, low)
    edge_y[0] = high.astype(BF16)
    edge_y[1] = low.astype(BF16)
    for k, (step, edge, halo, along) in enumerate(
        (
            (1, edge_x.at[0], halo_x.at[0], "team"),
            (-1, edge_x.at[1], halo_x.at[1], "team"),
            (1, edge_y.at[0], halo_y.at[0], "member"),
            (-1, edge_y.at[1], halo_y.at[1], "member"),
        )
    ):
        if along == "team":
            device = (lax.rem(team + step + teams, teams), member)
        else:
            device = (team, lax.rem(member + step + members, members))
        remote(edge, halo, send_h.at[k // 2], recv_h.at[k // 2], device)

    loads[3].wait()
    blocks_all = teams * members
    row = teams_ref[...]
    hits = (lax.broadcasted_iota(jnp.int32, (teams, blocks_all), 0) == row).astype(F32)
    ids = lax.broadcasted_iota(jnp.int32, (blocks_all, teams), 0)
    groups = lax.broadcasted_iota(jnp.int32, (blocks_all, teams), 1)
    inside = jnp.logical_and(ids >= groups * members, ids < (groups + 1) * members)
    tally = jnp.dot(hits.astype(BF16), inside.astype(F32).astype(BF16), preferred_element_type=F32)
    seconds_of = jnp.sum(jnp.where(tally > 1.5, 1.0, 0.0), axis=1, keepdims=True)
    most = jnp.max(seconds_of, axis=0, keepdims=True)
    flag_ref[...] = (most > extra + 0.5).astype(jnp.int32)

    for copy in loads[5:8]:
        copy.wait()
    nets = (w_in, w_mid, w_low, w_out, hidden_one, hidden_two, hidden_three)
    passed = {}

    def give(slot, d, target):
        remote(
            result.at[slot * (teams - 1) + d - 1],
            back.at[slot * teams + team],
            send_r,
            recv_r,
            (target, member),
        )

    def arrive(d):
        if d in place:
            held = rows[d] if d else rows[d].at[pl.ds(0, members - 1)]
            bytes_of(held, recv_b.at[place[d]])
        else:
            passed[d].wait_recv()
        second[d] = rows[d][picks[d][1]]

    def primary(unit):
        states = jnp.concatenate([rows[d][picks[d][0]] for d in unit], axis=1)
        rates = network_sum(states, *nets)
        for k, d in enumerate(unit):
            piece = rates[:, k * count : (k + 1) * count]
            if d:
                result[d - 1] = piece
                give(0, d, partner(team, d))
            else:
                back[team] = piece

    near = [d for d in range(min(2, teams))]
    for d in near:
        arrive(d)
    primary(near)
    evens = list(range(4, teams, 2))
    for d in evens + list(range(2, min(4, teams), 2)):
        arrive(d)
        passed[d + 1] = remote(
            rows[d], rows[d + 1], send_p.at[d // 2], recv_p.at[d // 2], (partner(team, 1), member)
        )
    for k in range(0, len(evens), 2):
        primary(evens[k : k + 2])
    for d in range(3, teams, 2):
        arrive(d)
    for start in range(0, extra, GROUP):
        spots = range(start, min(start + GROUP, extra))
        states = jnp.concatenate([second[sources[k]] for k in spots], axis=1)
        rates = network_sum(states, *nets)
        for k, spot in enumerate(spots):
            packed[spot] = rates[:, k * count : (k + 1) * count]
    for d in range(1, teams):
        result[teams + d - 2] = packed[rank_of[d]]
        give(1, d, partner(team, d))
    back[teams + team] = packed[rank_of[0]]
    odds = list(range(5, teams, 2))
    for k in range(0, len(odds), 2):
        primary(odds[k : k + 2])
    if teams > 2:
        primary([2, 3])

    for copy in loads[8:]:
        copy.wait()
    bytes_of(halo_x, recv_h.at[0])
    bytes_of(halo_y, recv_h.at[1])
    if extra < teams:
        flow_base(
            start_ref, section_ref, velocity_ref, spread_ref, halo_x, halo_y, base_ref
        )
    where = []
    for q in range(members):
        regime = team_of[0, team * members + q]
        rank = jnp.int32(0)
        for other in range(q):
            rank = rank + (team_of[0, team * members + other] == regime).astype(jnp.int32)
        where.append(jnp.minimum(rank, CAP - 1) * teams + regime)
    bytes_of(back.at[pl.ds(0, CAP * (teams - 1))], recv_r)
    for q in range(members):
        chosen[q] = back[where[q]]
    for e in range(members - 1, 0, -1):
        target = partner(member, e)
        remote(chosen.at[target], got.at[e - 1], send_m, recv_m, (team, target))
    total = chosen[member]
    bytes_of(got, recv_m)
    for e in range(members - 1):
        total = total + got[e]
    own_ref[...] = total
    for d in heads:
        bytes_of(rows[d] if d else rows[d].at[pl.ds(0, members - 1)], send_b.at[place[d]])
    for copy in passed.values():
        copy.wait_send()
    bytes_of(edge_x, send_h.at[0])
    bytes_of(edge_y, send_h.at[1])
    bytes_of(result, send_r)
    bytes_of(got, send_m)


def update_kernel(
    groups, cells_ref, rates_ref, base_ref, source_out, new_out, source_ref, new_ref, sems
):
    fields, rows_x, rows_y = base_ref.shape
    cells_x, cells_y = split_cells(cells_ref[...], rows_y)
    count = cells_x.shape[1]
    pick_x = row_mask(cells_x, rows_x)
    pick_y = (lax.broadcasted_iota(jnp.int32, (rows_y, count), 0) == cells_y).astype(F32)
    pick_y = pick_y.astype(BF16)
    pick_y = jnp.concatenate([pick_y, pick_y], axis=1)
    group = fields // groups
    for f in range(fields):
        spread_rates = jnp.where(pick_x, rates_ref[f : f + 1, :], 0.0)
        top = spread_rates.astype(BF16)
        rest = (spread_rates - top.astype(F32)).astype(BF16)
        source = lax.dot_general(
            jnp.concatenate([top, rest], axis=1),
            pick_y,
            (((1,), (1,)), ((), ())),
            preferred_element_type=F32,
        )
        source_ref[f] = source
        new_ref[f] = base_ref[f] + (0.25 * TIME_STEP) * source
        if (f + 1) % group == 0:
            span = pl.ds(f + 1 - group, group)
            for k, (held, out) in enumerate(((source_ref, source_out), (new_ref, new_out))):
                pltpu.make_async_copy(held.at[span], out.at[span], sems.at[k]).start()
    pltpu.make_async_copy(source_ref, source_out, sems.at[0]).wait()
    pltpu.make_async_copy(new_ref, new_out, sems.at[1]).wait()


def whole(space=VMEM):
    return pl.BlockSpec(memory_space=space)


def shards(
    state_start,
    state_section,
    velocity,
    diffusivity,
    flame_cells,
    block_team,
    w_in,
    w_mid,
    w_low,
    w_out,
):
    teams = lax.axis_size("team")
    members = lax.axis_size("member")
    fields, rows_x, rows_y = state_section.shape
    count = flame_cells.shape[1]
    dma = pltpu.SemaphoreType.DMA
    w_in = jnp.swapaxes(w_in, 2, 3)
    hidden = w_in.shape[3]
    wide = min(GROUP, teams) * count
    heads = len({d for d, _ in straight(teams, members)})
    operands = (
        state_section,
        state_start,
        velocity,
        flame_cells,
        block_team.reshape(1, -1),
        diffusivity,
        w_in,
        w_mid,
        w_low,
        w_out,
    )

    def networks(extra, collective, name, operands):
        return pl.pallas_call(
            functools.partial(fused_kernel, teams, members, extra),
            out_shape=(
                jax.ShapeDtypeStruct((fields, count), F32),
                jax.ShapeDtypeStruct(state_section.shape, F32),
                jax.ShapeDtypeStruct((1, 1), jnp.int32),
            ),
            in_specs=[whole(pltpu.HBM)] * len(operands),
            out_specs=(whole(), whole(), whole()),
            scratch_shapes=[
                VMEM(state_section.shape, F32),
                VMEM(state_start.shape, F32),
                VMEM(velocity.shape, F32),
                VMEM(flame_cells.shape, jnp.int32),
                VMEM((1, teams * members), jnp.int32),
                pltpu.SMEM((1, teams * members), jnp.int32),
                pltpu.SMEM(diffusivity.shape, F32),
                VMEM(w_in.shape, BF16),
                VMEM((hidden, fields), BF16),
                VMEM(w_mid.shape, BF16),
                VMEM(w_low.shape, BF16),
                VMEM(w_out.shape, BF16),
                VMEM((hidden, wide), BF16),
                VMEM((w_mid.shape[2], wide), BF16),
                VMEM((w_low.shape[2], wide), BF16),
                VMEM((teams, fields, count), BF16),
                VMEM((CAP * (teams - 1), fields, count), F32),
                VMEM((extra, fields, count), F32),
                VMEM((CAP * teams, fields, count), F32),
                VMEM((members, fields, count), F32),
                VMEM((members - 1, fields, count), F32),
                VMEM((2, fields, rows_y), BF16),
                VMEM((2, rows_x, rows_y), BF16),
                VMEM((2, fields, rows_y), BF16),
                VMEM((2, rows_x, rows_y), BF16),
                pltpu.SMEM((teams,), jnp.int32),
                dma((11,)),
                dma((heads,)),
                dma((heads,)),
                dma((-(-teams // 2),)),
                dma((-(-teams // 2),)),
                dma,
                dma,
                dma,
                dma,
                dma((2,)),
                dma((2,)),
            ]
            + [VMEM((members, fields, count), BF16)] * teams,
            compiler_params=pltpu.CompilerParams(
                collective_id=collective, has_side_effects=True, vmem_limit_bytes=GRANT
            ),
            name=name,
        )(*[pltpu.with_memory_space_constraint(x, pltpu.HBM) for x in operands])

    extra = max(2, teams // 4)
    rates, base, full = networks(extra, 0, "networks", operands)
    rates = lax.cond(
        full[0, 0] == 0,
        lambda rates, *operands: rates,
        lambda rates, *operands: networks(teams, 1, "general", operands)[0],
        rates,
        *operands,
    )
    groups = 6 if fields % 6 == 0 else fields
    return pl.pallas_call(
        functools.partial(update_kernel, groups),
        out_shape=(
            jax.ShapeDtypeStruct(state_section.shape, F32),
            jax.ShapeDtypeStruct(state_section.shape, F32),
        ),
        in_specs=[whole()] * 3,
        out_specs=(whole(pl.ANY), whole(pl.ANY)),
        scratch_shapes=[
            VMEM(state_section.shape, F32),
            VMEM(state_section.shape, F32),
            dma((2,)),
        ],
        compiler_params=pltpu.CompilerParams(vmem_limit_bytes=GRANT),
        name="update",
    )(flame_cells, rates, base)


def solution(mesh):
    grid = P(None, "team", "member")
    weights = P("team", "member", None, None)
    placed = (
        grid,
        grid,
        grid,
        P(),
        P(("team", "member"), None),
        P(),
        weights,
        weights,
        weights,
        weights,
    )
    return jax.shard_map(
        shards, mesh=mesh, in_specs=placed, out_specs=(grid, grid), check_vma=False
    )
```

```python
import functools

import jax
import jax.numpy as jnp
from jax import lax
from jax.experimental import pallas as pl
from jax.experimental.pallas import tpu as pltpu
from jax.sharding import PartitionSpec as P

CAP = 2
TIME_STEP = 0.25
GRANT = 24 << 20
GROUP = 4
FIRST = 4
MESH = pl.DeviceIdType.MESH
VMEM = pltpu.VMEM
F32 = jnp.float32
BF16 = jnp.bfloat16


def partner(index, flips):
    target = index
    bit = 1
    while bit <= flips:
        if flips & bit:
            target = target + bit - 2 * bit * lax.rem(index // bit, 2)
        bit *= 2
    return target


def split_cells(cells, rows_y):
    shift = rows_y.bit_length() - 1
    assert rows_y == 1 << shift
    return cells >> shift, cells & (rows_y - 1)


def row_mask(cells_x, rows_x):
    count = cells_x.shape[1]
    return lax.broadcasted_iota(jnp.int32, (rows_x, count), 0) == cells_x


def silu(x):
    half = 0.5 * x
    return half + half * jnp.tanh(half)


def straight(teams, members):
    far_first = range(members - 1, -1, -1)
    order = [(d, e) for e in far_first for d in range(min(2, teams)) if d or e]
    order += [(d, e) for e in far_first for d in range(4, teams, 2)]
    order += [(2, e) for e in far_first] if teams > 2 else []
    return order


def greeted(teams, members):
    order = straight(teams, members)
    return order + [(d, 0) for d in range(1, teams) if (d, 0) not in order]


def greet(team, member, teams, members):
    barrier = pltpu.get_barrier_semaphore()
    for d, e in greeted(teams, members):
        pl.semaphore_signal(
            barrier,
            inc=1,
            device_id=(partner(team, d), partner(member, e)),
            device_id_type=MESH,
        )
    return barrier


def flow_base(
    start_ref, section_ref, velocity_ref, spread_ref, halo_x_ref, halo_y_ref, base_ref
):
    fields, rows_x, rows_y = section_ref.shape
    lanes = lax.broadcasted_iota(jnp.int32, (rows_x, rows_y), 1)
    subs = lax.broadcasted_iota(jnp.int32, (rows_x, rows_y), 0)
    half_u = 0.5 * velocity_ref[0]
    half_v = 0.5 * velocity_ref[1]
    low_x = halo_x_ref[0].astype(F32)
    high_x = halo_x_ref[1].astype(F32)
    low_y = halo_y_ref[0].astype(F32)
    high_y = halo_y_ref[1].astype(F32)
    for f in range(fields):
        here = section_ref[f]
        plus_x = jnp.where(
            subs == rows_x - 1, high_x[f : f + 1], pltpu.roll(here, rows_x - 1, 0)
        )
        minus_x = jnp.where(subs == 0, low_x[f : f + 1], pltpu.roll(here, 1, 0))
        plus_y = jnp.where(
            lanes == rows_y - 1,
            pltpu.roll(high_y, rows_y - 1 - f, 1),
            pltpu.roll(here, rows_y - 1, 1),
        )
        edge = pltpu.roll(low_y, (rows_y - f) % rows_y, 1) if f else low_y
        minus_y = jnp.where(lanes == 0, edge, pltpu.roll(here, 1, 1))
        flow = (
            spread_ref[f] * (plus_x + minus_x + plus_y + minus_y - 4.0 * here)
            - half_u * (plus_x - minus_x)
            - half_v * (plus_y - minus_y)
        )
        base_ref[f] = 0.75 * start_ref[f] + 0.25 * (here + TIME_STEP * flow)


def network_sum(states, w_in, w_mid, w_low, w_out, hidden_one, hidden_two, hidden_three):
    count = states.shape[1]

    def layer(weight, source, target):
        total = weight.shape[0]
        half = -(-total // 32) * 16
        for start in range(0, total, half):
            size = min(half, total - start)
            out = jnp.dot(weight[start : start + size, :], source, preferred_element_type=F32)
            target[start : start + size, :count] = silu(out).astype(BF16)

    layer(w_in, states, hidden_one)
    layer(w_mid.at[0, 0], hidden_one[:, :count], hidden_two)
    layer(w_low.at[0, 0], hidden_two[:, :count], hidden_three)
    return jnp.dot(w_out[0, 0], hidden_three[:, :count], preferred_element_type=F32)


def fused_kernel(
    teams,
    members,
    extra,
    section_hbm,
    start_hbm,
    velocity_hbm,
    cells_hbm,
    teams_hbm,
    spread_hbm,
    w_in_hbm,
    w_mid_hbm,
    w_low_hbm,
    w_out_hbm,
    own_ref,
    base_ref,
    flag_ref,
    section_ref,
    start_ref,
    velocity_ref,
    cells_ref,
    teams_ref,
    team_of,
    spread_ref,
    w_in_raw,
    w_in,
    w_mid,
    w_low,
    w_out,
    hidden_one,
    hidden_two,
    hidden_three,
    second,
    result,
    packed,
    back,
    chosen,
    got,
    edge_x,
    edge_y,
    halo_x,
    halo_y,
    rank_of,
    load_sem,
    send_b,
    recv_b,
    send_p,
    recv_p,
    send_r,
    recv_r,
    send_m,
    recv_m,
    send_h,
    recv_h,
    *rows,
):
    team = lax.axis_index("team")
    member = lax.axis_index("member")
    loads = []
    for k, (source, target) in enumerate(
        (
            (cells_hbm, cells_ref),
            (section_hbm, section_ref),
            (teams_hbm, team_of),
            (teams_hbm, teams_ref),
            (w_in_hbm, w_in_raw),
            (w_mid_hbm, w_mid),
            (w_low_hbm, w_low),
            (w_out_hbm, w_out),
            (spread_hbm, spread_ref),
            (velocity_hbm, velocity_ref),
            (start_hbm, start_ref),
        )
    ):
        copy = pltpu.make_async_copy(source, target, load_sem.at[k])
        if k < FIRST:
            copy.start()
        loads.append(copy)
    barrier = greet(team, member, teams, members)
    fields, rows_x, rows_y = section_ref.shape
    loads[0].wait()
    cells_x, cells_y = split_cells(cells_ref[...], rows_y)
    count = cells_x.shape[1]
    pick_y = (lax.broadcasted_iota(jnp.int32, (rows_y, count), 0) == cells_y).astype(F32)
    pick_x = row_mask(cells_x, rows_x)
    loads[1].wait()
    for copy in loads[FIRST:]:
        copy.start()
    flat = section_ref[...].reshape(fields * rows_x, rows_y).astype(BF16)
    taken = jnp.dot(flat, pick_y.astype(BF16), preferred_element_type=F32)
    taken = taken.reshape(fields, rows_x, count)
    own = jnp.sum(jnp.where(pick_x[None], taken, 0.0), axis=1)
    rows[0][member] = own.astype(BF16)
    pl.semaphore_wait(barrier, len(greeted(teams, members)))

    def bytes_of(ref, semaphore):
        pltpu.make_async_copy(ref, ref, semaphore).wait()

    def remote(source, target, send, recv, device):
        copy = pltpu.make_async_remote_copy(
            src_ref=source,
            dst_ref=target,
            send_sem=send,
            recv_sem=recv,
            device_id=device,
            device_id_type=MESH,
        )
        copy.start()
        return copy

    direct = {}
    heads = sorted({d for d, _ in straight(teams, members)})
    place = {d: k for k, d in enumerate(heads)}
    for d, e in straight(teams, members):
        direct[d, e] = remote(
            rows[0].at[member],
            rows[d].at[member],
            send_b.at[place[d]],
            recv_b.at[place[d]],
            (partner(team, d), partner(member, e)),
        )

    edge_x[0] = section_ref[:, rows_x - 1, :].astype(BF16)
    edge_x[1] = section_ref[:, 0, :].astype(BF16)
    loads[2].wait()
    picks = []
    found = jnp.int32(0)
    sources = [jnp.int32(0)] * extra
    for d in range(teams):
        base = partner(team, d) * members
        first = jnp.int32(0)
        later = jnp.int32(0)
        held = jnp.int32(0)
        for q in range(members - 1, -1, -1):
            here = team_of[0, base + q] == team
            later = jnp.where(here, first, later)
            first = jnp.where(here, q, first)
            held = held + here.astype(jnp.int32)
        picks.append((first, later))
        if extra < teams:
            twice = held > 1
            rank_of[d] = jnp.minimum(found, extra - 1)
            for k in range(extra):
                sources[k] = jnp.where(
                    jnp.logical_and(twice, found == k), jnp.int32(d), sources[k]
                )
            found = found + twice.astype(jnp.int32)
        else:
            rank_of[d] = jnp.int32(d)
            sources[d] = jnp.int32(d)
    loads[4].wait()
    w_in[...] = w_in_raw[0, 0].T
    lanes = lax.broadcasted_iota(jnp.int32, (rows_x, rows_y), 1)
    low = jnp.zeros((rows_x, rows_y), F32)
    high = jnp.zeros((rows_x, rows_y), F32)
    for f in range(fields):
        plane = section_ref[f]
        here = lanes == f
        high = jnp.where(here, pltpu.roll(plane, (f + 1) % rows_y, 1), high)
        low = jnp.where(here, pltpu.roll(plane, f, 1) if f else plane, low)
    edge_y[0] = high.astype(BF16)
    edge_y[1] = low.astype(BF16)
    for k, (step, edge, halo, along) in enumerate(
        (
            (1, edge_x.at[0], halo_x.at[0], "team"),
            (-1, edge_x.at[1], halo_x.at[1], "team"),
            (1, edge_y.at[0], halo_y.at[0], "member"),
            (-1, edge_y.at[1], halo_y.at[1], "member"),
        )
    ):
        if along == "team":
            device = (lax.rem(team + step + teams, teams), member)
        else:
            device = (team, lax.rem(member + step + members, members))
        remote(edge, halo, send_h.at[k // 2], recv_h.at[k // 2], device)

    loads[3].wait()
    blocks_all = teams * members
    row = teams_ref[...]
    hits = (lax.broadcasted_iota(jnp.int32, (teams, blocks_all), 0) == row).astype(F32)
    ids = lax.broadcasted_iota(jnp.int32, (blocks_all, teams), 0)
    groups = lax.broadcasted_iota(jnp.int32, (blocks_all, teams), 1)
    inside = jnp.logical_and(ids >= groups * members, ids < (groups + 1) * members)
    tally = jnp.dot(hits.astype(BF16), inside.astype(F32).astype(BF16), preferred_element_type=F32)
    seconds_of = jnp.sum(jnp.where(tally > 1.5, 1.0, 0.0), axis=1, keepdims=True)
    most = jnp.max(seconds_of, axis=0, keepdims=True)
    flag_ref[...] = (most > extra + 0.5).astype(jnp.int32)

    for copy in loads[5:8]:
        copy.wait()
    nets = (w_in, w_mid, w_low, w_out, hidden_one, hidden_two, hidden_three)
    passed = {}

    def give(slot, d, target):
        remote(
            result.at[slot * (teams - 1) + d - 1],
            back.at[slot * teams + team],
            send_r,
            recv_r,
            (target, member),
        )

    def arrive(d):
        if d in place:
            held = rows[d] if d else rows[d].at[pl.ds(0, members - 1)]
            bytes_of(held, recv_b.at[place[d]])
        else:
            passed[d].wait_recv()
        second[d] = rows[d][picks[d][1]]

    def primary(unit):
        states = jnp.concatenate([rows[d][picks[d][0]] for d in unit], axis=1)
        rates = network_sum(states, *nets)
        for k, d in enumerate(unit):
            piece = rates[:, k * count : (k + 1) * count]
            if d:
                result[d - 1] = piece
                give(0, d, partner(team, d))
            else:
                back[team] = piece

    near = [d for d in range(min(2, teams))]
    for d in near:
        arrive(d)
    primary(near)
    evens = list(range(4, teams, 2))
    for d in evens + list(range(2, min(4, teams), 2)):
        arrive(d)
        passed[d + 1] = remote(
            rows[d], rows[d + 1], send_p.at[d // 2 - 1], recv_p.at[d // 2 - 1], (partner(team, 1), member)
        )
    for k in range(0, len(evens), 2):
        primary(evens[k : k + 2])
    for d in range(3, teams, 2):
        arrive(d)
    for start in range(0, extra, GROUP):
        spots = range(start, min(start + GROUP, extra))
        states = jnp.concatenate([second[sources[k]] for k in spots], axis=1)
        rates = network_sum(states, *nets)
        for k, spot in enumerate(spots):
            packed[spot] = rates[:, k * count : (k + 1) * count]
    for d in range(1, teams):
        result[teams + d - 2] = packed[rank_of[d]]
        give(1, d, partner(team, d))
    back[teams + team] = packed[rank_of[0]]
    odds = list(range(5, teams, 2))
    for k in range(0, len(odds), 2):
        primary(odds[k : k + 2])
    if teams > 2:
        primary([2, 3])

    for copy in loads[8:]:
        copy.wait()
    bytes_of(halo_x, recv_h.at[0])
    bytes_of(halo_y, recv_h.at[1])
    if extra < teams:
        flow_base(
            start_ref, section_ref, velocity_ref, spread_ref, halo_x, halo_y, base_ref
        )
    where = []
    for q in range(members):
        regime = team_of[0, team * members + q]
        rank = jnp.int32(0)
        for other in range(q):
            rank = rank + (team_of[0, team * members + other] == regime).astype(jnp.int32)
        where.append(jnp.minimum(rank, CAP - 1) * teams + regime)
    bytes_of(back.at[pl.ds(0, CAP * (teams - 1))], recv_r)
    for q in range(members):
        chosen[q] = back[where[q]]
    for e in range(members - 1, 0, -1):
        target = partner(member, e)
        remote(chosen.at[target], got.at[e - 1], send_m, recv_m, (team, target))
    total = chosen[member]
    bytes_of(got, recv_m)
    for e in range(members - 1):
        total = total + got[e]
    own_ref[...] = total
    for d in heads:
        bytes_of(rows[d] if d else rows[d].at[pl.ds(0, members - 1)], send_b.at[place[d]])
    for copy in passed.values():
        copy.wait_send()
    bytes_of(edge_x, send_h.at[0])
    bytes_of(edge_y, send_h.at[1])
    bytes_of(result, send_r)
    bytes_of(got, send_m)


def update_kernel(
    groups, cells_ref, rates_ref, base_ref, source_out, new_out, source_ref, new_ref, sems
):
    fields, rows_x, rows_y = base_ref.shape
    cells_x, cells_y = split_cells(cells_ref[...], rows_y)
    count = cells_x.shape[1]
    pick_x = row_mask(cells_x, rows_x)
    pick_y = (lax.broadcasted_iota(jnp.int32, (rows_y, count), 0) == cells_y).astype(F32)
    pick_y = pick_y.astype(BF16)
    pick_y = jnp.concatenate([pick_y, pick_y], axis=1)
    group = fields // groups
    for f in range(fields):
        spread_rates = jnp.where(pick_x, rates_ref[f : f + 1, :], 0.0)
        top = spread_rates.astype(BF16)
        rest = (spread_rates - top.astype(F32)).astype(BF16)
        source = lax.dot_general(
            jnp.concatenate([top, rest], axis=1),
            pick_y,
            (((1,), (1,)), ((), ())),
            preferred_element_type=F32,
        )
        source_ref[f] = source
        new_ref[f] = base_ref[f] + (0.25 * TIME_STEP) * source
        if (f + 1) % group == 0:
            span = pl.ds(f + 1 - group, group)
            for k, (held, out) in enumerate(((source_ref, source_out), (new_ref, new_out))):
                pltpu.make_async_copy(held.at[span], out.at[span], sems.at[k]).start()
    pltpu.make_async_copy(source_ref, source_out, sems.at[0]).wait()
    pltpu.make_async_copy(new_ref, new_out, sems.at[1]).wait()


def whole(space=VMEM):
    return pl.BlockSpec(memory_space=space)


def shards(
    state_start,
    state_section,
    velocity,
    diffusivity,
    flame_cells,
    block_team,
    w_in,
    w_mid,
    w_low,
    w_out,
):
    teams = lax.axis_size("team")
    members = lax.axis_size("member")
    fields, rows_x, rows_y = state_section.shape
    count = flame_cells.shape[1]
    dma = pltpu.SemaphoreType.DMA
    w_in = jnp.swapaxes(w_in, 2, 3)
    hidden = w_in.shape[3]
    wide = min(GROUP, teams) * count
    heads = len({d for d, _ in straight(teams, members)})
    operands = (
        state_section,
        state_start,
        velocity,
        flame_cells,
        block_team.reshape(1, -1),
        diffusivity,
        w_in,
        w_mid,
        w_low,
        w_out,
    )

    def networks(extra, collective, name, operands):
        return pl.pallas_call(
            functools.partial(fused_kernel, teams, members, extra),
            out_shape=(
                jax.ShapeDtypeStruct((fields, count), F32),
                jax.ShapeDtypeStruct(state_section.shape, F32),
                jax.ShapeDtypeStruct((1, 1), jnp.int32),
            ),
            in_specs=[whole(pltpu.HBM)] * len(operands),
            out_specs=(whole(), whole(), whole()),
            scratch_shapes=[
                VMEM(state_section.shape, F32),
                VMEM(state_start.shape, F32),
                VMEM(velocity.shape, F32),
                VMEM(flame_cells.shape, jnp.int32),
                VMEM((1, teams * members), jnp.int32),
                pltpu.SMEM((1, teams * members), jnp.int32),
                pltpu.SMEM(diffusivity.shape, F32),
                VMEM(w_in.shape, BF16),
                VMEM((hidden, fields), BF16),
                VMEM(w_mid.shape, BF16),
                VMEM(w_low.shape, BF16),
                VMEM(w_out.shape, BF16),
                VMEM((hidden, wide), BF16),
                VMEM((w_mid.shape[2], wide), BF16),
                VMEM((w_low.shape[2], wide), BF16),
                VMEM((teams, fields, count), BF16),
                VMEM((CAP * (teams - 1), fields, count), F32),
                VMEM((extra, fields, count), F32),
                VMEM((CAP * teams, fields, count), F32),
                VMEM((members, fields, count), F32),
                VMEM((members - 1, fields, count), F32),
                VMEM((2, fields, rows_y), BF16),
                VMEM((2, rows_x, rows_y), BF16),
                VMEM((2, fields, rows_y), BF16),
                VMEM((2, rows_x, rows_y), BF16),
                pltpu.SMEM((teams,), jnp.int32),
                dma((11,)),
                dma((heads,)),
                dma((heads,)),
                dma((max(1, teams // 2 - 1),)),
                dma((max(1, teams // 2 - 1),)),
                dma,
                dma,
                dma,
                dma,
                dma((2,)),
                dma((2,)),
            ]
            + [VMEM((members, fields, count), BF16)] * teams,
            compiler_params=pltpu.CompilerParams(
                collective_id=collective, has_side_effects=True, vmem_limit_bytes=GRANT
            ),
            name=name,
        )(*[pltpu.with_memory_space_constraint(x, pltpu.HBM) for x in operands])

    extra = max(2, teams // 4)
    rates, base, full = networks(extra, 0, "networks", operands)
    rates = lax.cond(
        full[0, 0] == 0,
        lambda rates, *operands: rates,
        lambda rates, *operands: networks(teams, 1, "general", operands)[0],
        rates,
        *operands,
    )
    groups = 6 if fields % 6 == 0 else fields
    return pl.pallas_call(
        functools.partial(update_kernel, groups),
        out_shape=(
            jax.ShapeDtypeStruct(state_section.shape, F32),
            jax.ShapeDtypeStruct(state_section.shape, F32),
        ),
        in_specs=[whole()] * 3,
        out_specs=(whole(pl.ANY), whole(pl.ANY)),
        scratch_shapes=[
            VMEM(state_section.shape, F32),
            VMEM(state_section.shape, F32),
            dma((2,)),
        ],
        compiler_params=pltpu.CompilerParams(vmem_limit_bytes=GRANT),
        name="update",
    )(flame_cells, rates, base)


def solution(mesh):
    grid = P(None, "team", "member")
    weights = P("team", "member", None, None)
    placed = (
        grid,
        grid,
        grid,
        P(),
        P(("team", "member"), None),
        P(),
        weights,
        weights,
        weights,
        weights,
    )
    return jax.shard_map(
        shards, mesh=mesh, in_specs=placed, out_specs=(grid, grid), check_vma=False
    )
```
